32 devices in a mesh: groups: 2 (over y), row: 8 (over z, x), col: 2 (over core).
Axes of the slice: x: 2, y: 2, z: 4, core: 2. Of those that a mesh axis runs over, the one named last changes fastest.
Arguments:
- sigma_anc: bfloat16 [16384, 8192], P(('groups', 'row'), 'col'), parts along dimension 0, as said below
- panel: bfloat16 [16384, 3072], P(('groups', 'row'), 'col'), parts along dimension 0
- holder: int32 [128], P('groups'), parts along dimension 0, may hold values from 0 to 63, each once
- dinv_diag: float32 [6144], P(('groups', 'col')), parts along dimension 0, may hold values from 0.5 to 2
Outputs:
- sigma_aj: bfloat16 [16384, 3072], P(('groups', 'row'), 'col'), parts along dimension 0
- variances: float32 [6144], P(('groups', 'col')), parts along dimension 0
The draws below stay inside these ranges and needn't reach their ends.
There are 2 independent parts, one for each index of `groups`. The reference program is written for one: setup_inputs(seed, part) draws one part's arguments, and reference() takes and returns one part's arrays. A program takes and returns all parts, laid end to end along the dimension named above; each array names one. Nothing has to cross between parts.
Inputs may be any that keep to these rules, and one draw needn't show every extreme that they name: holder is a permutation of the 64 tiles. sigma_anc is symmetric and positive definite.
All inputs are finite; a program needn't handle non-finite values.
Results may differ from the reference program's by a relative error of at most 0.001.
Values may be sent and summed in bfloat16 or wider, within the bound.
A program may use at most 128 MiB of HBM per device.

```python
import math
import jax
import jax.numpy as jnp

A = 8192
S = 3072
TILE = 128
TILES = 64


def draw_sigma_anc(key, part):
    kone = jax.random.fold_in(key, 11)
    ktwo = jax.random.fold_in(key, 12)
    base = jax.random.normal(kone, (A, A), jnp.float32)
    sym = (base + base.T) * (0.5 / jnp.sqrt(jnp.float32(A)))
    diag = jax.random.uniform(ktwo, (A,), jnp.float32, 1.5, 3.0)
    return (sym + jnp.diag(diag)).astype(jnp.bfloat16)


def draw_panel(key, part):
    kone = jax.random.fold_in(key, 21)
    ktwo = jax.random.fold_in(key, 22)
    rows = jnp.arange(A, dtype=jnp.float32) / A
    row_scale = 10.0 ** (rows - 0.5)
    col_scale = 10.0 ** jax.random.uniform(ktwo, (S,), jnp.float32, -0.5, 0.5)
    entries = jax.random.normal(kone, (A, S), jnp.float32)
    vals = entries * row_scale[:, None] * col_scale[None, :] / jnp.sqrt(jnp.float32(A))
    return vals.astype(jnp.bfloat16)


def block_levels(stream_key, shape, split, least, largest):
    def one(position, parts):
        heights = jax.random.uniform(jax.random.fold_in(jax.random.fold_in(stream_key, 6), position), (parts,), jnp.float32, least / len(split), largest / len(split))
        return jnp.repeat(jnp.exp(heights), shape[position] // parts).reshape((-1,) + (1,) * (len(shape) - position - 1))

    loudness = one(*split[0])
    for cut in split[1:]:
        loudness = loudness * one(*cut)
    return loudness


def setup_inputs(seed: int = 0, part: int = 0) -> dict:
    key_of = jax.random.split(jax.random.key(seed), 5)
    part_keys = jax.random.split(jax.random.fold_in(key_of[4], part), 5)
    return {
        "sigma_anc": draw_sigma_anc(jax.random.fold_in(jax.random.fold_in(key_of[4], part), 71), part),
        "panel": draw_panel(jax.random.fold_in(jax.random.fold_in(key_of[4], part), 71), part),
        "holder": jax.random.permutation(part_keys[2], TILES).astype(jnp.int32),
        "dinv_diag": jnp.clip(jnp.exp(math.log(2.0) - 1.3862944 * jax.random.uniform(part_keys[3], (S,), jnp.float32) ** block_levels(part_keys[3], (S,), ((0, 2),), -0.2, 0.2)), 0.5, 2.0),
    }


def reference(sigma_anc, panel, holder, dinv_diag):
    tiles = panel.reshape(TILES, TILE, S)
    panel_log = jnp.take(tiles, holder.astype(jnp.int32), axis=0).reshape(A, S)
    prod = jnp.dot(sigma_anc, panel_log, preferred_element_type=jnp.float32)
    sigma_aj = (-prod).astype(jnp.bfloat16)
    variances = dinv_diag + jnp.sum(panel_log.astype(jnp.float32) * prod, axis=0)
    return sigma_aj, variances
```

```python
import functools

import jax
import jax.numpy as jnp
from jax import lax
from jax.experimental import pallas as pl
from jax.experimental.pallas import tpu as pltpu
from jax.sharding import PartitionSpec as P

MESH = pl.DeviceIdType.MESH


def block_of(size, most):
    block = min(size, most)
    while size % block:
        block -= 128
    return block


def kernel(n, nc, holder, logical, sigma, panel, out, sums, s, p, acc, staged, parts,
           own_sem, far_sem, near_sem, f_send, f_recv, b_send, b_recv, o_sem, v_send, v_recv):
    g = lax.axis_index("groups")
    r = lax.axis_index("row")
    c = lax.axis_index("col")
    per, tile, cols = panel.shape
    rows, width = sigma.shape
    tiles = p.shape[0]
    half = n // 2
    fwd = (per + 1) // 2
    bwd = per - fwd

    def row_of(at):
        at = lax.rem(at + 2 * n, n)
        odd = at // half
        return 2 * (at + odd * (2 * half - 1 - 2 * at)) + odd

    odd = lax.rem(r, 2)
    up = r // 2
    at = up + odd * (2 * half - 1 - 2 * up)
    after = (g, row_of(at + 1), c)
    before = (g, row_of(at - 1), c)

    barrier = pltpu.get_barrier_semaphore()

    def greet(k, carry):
        pl.semaphore_signal(barrier, 1, device_id=(g, lax.rem(r + k, n), c), device_id_type=MESH)
        return carry

    lax.fori_loop(1, n, greet, 0)
    for k in range(1, nc):
        pl.semaphore_signal(barrier, 1, device_id=(g, r, lax.rem(c + k, nc)), device_id_type=MESH)
    pl.semaphore_wait(barrier, n - 1 + nc - 1)

    def f_tile(k, i):
        return row_of(at - k) * per + i

    def b_tile(k, i):
        return row_of(at + k) * per + fwd + i

    def f_copy(k, i, src=None):
        t = f_tile(k, i)
        return pltpu.make_async_remote_copy(
            src_ref=p.at[t] if src is None else src, dst_ref=p.at[t],
            send_sem=f_send.at[k * fwd + i], recv_sem=f_recv.at[k * fwd + i],
            device_id=after, device_id_type=MESH)

    def b_copy(k, i, src=None):
        t = b_tile(k, i)
        return pltpu.make_async_remote_copy(
            src_ref=p.at[t] if src is None else src, dst_ref=p.at[t],
            send_sem=b_send.at[k * bwd + i], recv_sem=b_recv.at[k * bwd + i],
            device_id=before, device_id_type=MESH)

    def f_landed(k, i):
        t = f_tile(k, i)
        return pltpu.make_async_remote_copy(
            src_ref=p.at[t], dst_ref=p.at[t],
            send_sem=f_send.at[(k - 1) * fwd + i], recv_sem=f_recv.at[(k - 1) * fwd + i],
            device_id=after, device_id_type=MESH)

    def b_landed(k, i):
        t = b_tile(k, i)
        return pltpu.make_async_remote_copy(
            src_ref=p.at[t], dst_ref=p.at[t],
            send_sem=b_send.at[(k - 1) * bwd + i], recv_sem=b_recv.at[(k - 1) * bwd + i],
            device_id=before, device_id_type=MESH)

    for i in range(fwd):
        f_copy(0, i, panel.at[i]).start()
        if i < bwd:
            b_copy(0, i, panel.at[fwd + i]).start()

    held = width // tile

    def near(j):
        return pltpu.make_async_copy(
            sigma.at[:, pl.ds(pl.multiple_of(j * tile, tile), tile)], s.at[c * held + j], near_sem.at[j])

    def far(k, j):
        return pltpu.make_async_remote_copy(
            src_ref=sigma.at[:, pl.ds(pl.multiple_of(j * tile, tile), tile)], dst_ref=s.at[c * held + j],
            send_sem=far_sem.at[2 * k - 2, j], recv_sem=far_sem.at[2 * k - 1, j],
            device_id=(g, r, lax.rem(c + k, nc)), device_id_type=MESH)

    def far_landed(k, j):
        t = lax.rem(c + nc - k, nc) * held + j
        return pltpu.make_async_remote_copy(
            src_ref=s.at[t], dst_ref=s.at[t],
            send_sem=far_sem.at[2 * k - 2, j], recv_sem=far_sem.at[2 * k - 1, j],
            device_id=(g, r, lax.rem(c + k, nc)), device_id_type=MESH)

    def each(low, high, act):
        def step(k, carry):
            act(k)
            return carry
        lax.fori_loop(low, high, step, 0)

    for k in range(1, nc):
        each(0, held, lambda j: far(k, j).start())
    each(0, held, lambda j: near(j).start())
    own = pltpu.make_async_copy(panel, p.at[pl.ds(r * per, per)], own_sem)
    own.start()
    acc[...] = jnp.zeros_like(acc)
    own.wait()
    each(0, held, lambda j: near(j).wait())
    for k in range(1, nc):
        each(0, held, lambda j: far_landed(k, j).wait_recv())

    rb = block_of(rows, 512)
    cb = block_of(cols, 512)
    across = cols // cb

    def multiply(slots):
        columns = [logical[t] for t in slots]

        def block(q, carry):
            rs = pl.ds(pl.multiple_of((q // across) * rb, rb), rb)
            cs = pl.ds(pl.multiple_of(lax.rem(q, across) * cb, cb), cb)
            lhs = jnp.concatenate([s[w, rs, :] for w in columns], axis=1)
            rhs = jnp.concatenate([p[t, :, cs] for t in slots], axis=0)
            acc[rs, cs] += jnp.dot(lhs, rhs, preferred_element_type=jnp.float32)
            return carry

        lax.fori_loop(0, (rows // rb) * across, block, 0)

    def unit(u, carry):
        k = u // fwd
        i = lax.rem(u, fwd)

        @pl.when(k > 0)
        def _():
            f_landed(k, i).wait_recv()

            @pl.when(k < n - 1)
            def _():
                f_copy(k, i).start()

        if bwd == fwd:
            @pl.when(k > 0)
            def _():
                b_landed(k, i).wait_recv()

                @pl.when(k < n - 1)
                def _():
                    b_copy(k, i).start()

            multiply([f_tile(k, i), b_tile(k, i)])
        else:
            multiply([f_tile(k, i)])
            if bwd:
                @pl.when(i < bwd)
                def _():
                    @pl.when(k > 0)
                    def _():
                        b_landed(k, i).wait_recv()

                        @pl.when(k < n - 1)
                        def _():
                            b_copy(k, i).start()

                    multiply([b_tile(k, i)])
        return carry

    lax.fori_loop(0, n * fwd, unit, 0)

    parts[r] = jnp.zeros((1, cols), jnp.float32)

    def weigh(j, carry):
        where = pl.ds(pl.multiple_of(j * tile, tile), tile)
        mine = p[holder[r * per + j]]
        for b in range(across):
            cs = pl.ds(b * cb, cb)
            term = mine[:, b * cb:(b + 1) * cb].astype(jnp.float32) * acc[where, cs]
            parts[r, :, cs] += jnp.sum(term, axis=0, keepdims=True)
        return carry

    lax.fori_loop(0, per, weigh, 0)

    def share(k):
        to = lax.rem(r + k, n)
        return pltpu.make_async_remote_copy(
            src_ref=parts.at[r], dst_ref=parts.at[r],
            send_sem=v_send.at[k - 1], recv_sem=v_recv.at[k - 1],
            device_id=(g, to, c), device_id_type=MESH)

    def gone(k):
        frm = lax.rem(r + n - k, n)
        return pltpu.make_async_remote_copy(
            src_ref=parts.at[frm], dst_ref=parts.at[frm],
            send_sem=v_send.at[k - 1], recv_sem=v_recv.at[k - 1],
            device_id=(g, lax.rem(r + k, n), c), device_id_type=MESH)

    each(1, n, lambda k: share(k).start())

    def put(j):
        where = pl.ds(pl.multiple_of(j * tile, tile), tile)
        return pltpu.make_async_copy(staged.at[where], out.at[where], o_sem.at[j])

    def finish(j, carry):
        where = pl.ds(pl.multiple_of(j * tile, tile), tile)
        staged[where, :] = (-acc[where, :]).astype(staged.dtype)
        put(j).start()
        return carry

    lax.fori_loop(0, per, finish, 0)

    for k in range(1, nc):
        each(0, held, lambda j: far(k, j).wait_send())
    each(0, (n - 1) * fwd, lambda u: f_copy(u // fwd, lax.rem(u, fwd)).wait_send())
    if bwd:
        each(0, (n - 1) * bwd, lambda u: b_copy(u // bwd, lax.rem(u, bwd)).wait_send())
    each(0, per, lambda j: put(j).wait())
    each(1, n, lambda k: gone(k).wait_recv())
    each(1, n, lambda k: share(k).wait_send())
    total = parts[0]
    for k in range(1, n):
        total += parts[k]
    sums[...] = total


def ladder(n, nc, wide, split, spare, kept, holder, logical, sigma, panel, out, sums,
           s, acc, staged, ef, accf, across, along, parts,
           far_sem, near_sem, own_sem, p_send, p_recv, u_send, u_recv, w_send, w_recv,
           t_send, t_recv, y_send, y_recv, e_send, e_recv, o_sem, v_send, v_recv, *bufs):
    g = lax.axis_index("groups")
    r = lax.axis_index("row")
    c = lax.axis_index("col")
    per, tile, cols = panel.shape
    rows, width = sigma.shape
    chunks = cols // wide
    ps, ses = bufs[:chunks], bufs[chunks:]
    held = width // tile
    grp = per // split
    steps = chunks * split
    late = spare * split
    z = r // 2
    x = lax.rem(r, 2)
    xb = 1 - x
    side = z // 2
    ze, zm, zo, zf = 3 * side, 1 + side, 2 - side, 3 - 3 * side
    edge = 2 * ze + x

    def at(zz, xx):
        return 2 * zz + xx

    def dev(zz, xx):
        return (g, 2 * zz + xx, c)

    twin = (g, r, 1 - c)

    barrier = pltpu.get_barrier_semaphore()

    def greet(k, carry):
        pl.semaphore_signal(barrier, 1, device_id=(g, lax.rem(r + k, n), c), device_id_type=MESH)
        return carry

    lax.fori_loop(1, n, greet, 0)
    pl.semaphore_signal(barrier, 1, device_id=twin, device_id_type=MESH)
    pl.semaphore_wait(barrier, n)

    def each(low, high, act):
        def step(k, carry):
            act(k)
            return carry
        lax.fori_loop(low, high, step, 0)

    def piece(block, i):
        return ps[i // split].at[pl.ds(block * per + (i % split) * grp, grp)]

    def first(i):
        return panel.at[pl.ds((i % split) * grp, grp), :, pl.ds((i // split) * wide, wide)]

    def move(block, i, to, way, src=None):
        return pltpu.make_async_remote_copy(
            src_ref=piece(block, i) if src is None else src, dst_ref=piece(block, i),
            send_sem=p_send.at[block, way, i], recv_sem=p_recv.at[block, i],
            device_id=to, device_id_type=MESH)

    def near(j):
        return pltpu.make_async_copy(
            sigma.at[:, pl.ds(pl.multiple_of(j * tile, tile), tile)], s.at[c * held + j], near_sem.at[j])

    def far(j):
        return pltpu.make_async_remote_copy(
            src_ref=sigma.at[:, pl.ds(pl.multiple_of(j * tile, tile), tile)], dst_ref=s.at[c * held + j],
            send_sem=far_sem.at[0, j], recv_sem=far_sem.at[1, j], device_id=twin, device_id_type=MESH)

    def far_landed(j):
        t = (1 - c) * held + j
        return pltpu.make_async_remote_copy(
            src_ref=s.at[t], dst_ref=s.at[t],
            send_sem=far_sem.at[0, j], recv_sem=far_sem.at[1, j], device_id=twin, device_id_type=MESH)

    def own(q):
        return pltpu.make_async_copy(
            panel.at[:, :, pl.ds(q * wide, wide)], ps[q].at[pl.ds(r * per, per)], own_sem.at[q])

    def load_sigma():
        each(0, held, lambda j: far(j).start())
        each(0, held, lambda j: near(j).start())
        for q in range(chunks):
            own(q).start()

    def have_sigma():
        each(0, held, lambda j: near(j).wait())
        each(0, held, lambda j: far_landed(j).wait_recv())
        for q in range(chunks):
            own(q).wait()
        parts[r] = jnp.zeros((1, cols), jnp.float32)

    rb = block_of(rows, 512)

    def multiply(i):
        q, h = i // split, i % split
        if h == 0:
            acc[...] = jnp.zeros_like(acc)
        downs = rows // rb

        def block(u, carry):
            pair = u // downs
            rs = pl.ds(pl.multiple_of(lax.rem(u, downs) * rb, rb), rb)
            slots = [(2 * pair + m) * per + h * grp + j for m in range(2) for j in range(grp)]
            lhs = jnp.concatenate([s[logical[t], rs, :] for t in slots], axis=1)
            rhs = jnp.concatenate([ps[q][t] for t in slots], axis=0)
            acc[rs, :] += jnp.dot(lhs, rhs, preferred_element_type=jnp.float32)
            return carry

        lax.fori_loop(0, (n // 2) * downs, block, 0)

    def put(q):
        return pltpu.make_async_copy(
            staged.at[q % 2], out.at[:, pl.ds(q * wide, wide)], o_sem.at[q])

    def finish(q, waited):
        cs = pl.ds(q * wide, wide)

        if waited is not None:
            put(waited).wait()

        def weigh(j, carry):
            where = pl.ds(pl.multiple_of(j * tile, tile), tile)
            prod = acc[where, :]
            staged[q % 2, where, :] = (-prod).astype(staged.dtype)
            term = ps[q][holder[r * per + j]].astype(jnp.float32) * prod
            parts[r, :, cs] += jnp.sum(term, axis=0, keepdims=True)
            return carry

        lax.fori_loop(0, per, weigh, 0)
        put(q).start()

    def rel(idx):
        zz = idx // 2
        base = jnp.where(zz == 0, 1, jnp.where(zz == 1, 2, jnp.where(zz == 2, 0, 3)))
        return 2 * (base + side * (3 - 2 * base)) + lax.rem(x + idx, 2)

    same = [(k, d) for k in range(per) for d in (([1] if k >= kept else []) + [4, 5])]
    other = [(k, d) for k in range(per) for d in (([2] if k >= kept else []) + [3, 6, 7])]
    quota = -(-max(len(same), len(other)) // (steps + 1))

    def turn(u):
        return min(u // quota, steps)

    def unit(k, d, to):
        b = rel(d)
        return pltpu.make_async_remote_copy(
            src_ref=sigma.at[pl.ds(k * tile, tile), pl.ds(pl.multiple_of((b - c * (n // nc)) * rows, rows), rows)],
            dst_ref=ses[k].at[:, pl.ds(pl.multiple_of(b * rows, rows), rows)],
            send_sem=u_send.at[k, d], recv_sem=u_recv.at[k, d], device_id=to, device_id_type=MESH)

    def pass_on(k, d):
        b = rel(d)
        ref = ses[k].at[:, pl.ds(pl.multiple_of(b * rows, rows), rows)]
        return pltpu.make_async_remote_copy(
            src_ref=ref, dst_ref=ref, send_sem=w_send.at[k, d], recv_sem=w_recv.at[k, d],
            device_id=twin, device_id_type=MESH)

    def by_core(act):
        @pl.when(c == side)
        def _():
            act(same, other)

        @pl.when(c != side)
        def _():
            act(other, same)

    half = rows // nc

    def lend(k, way):
        dst = (across, along)[way].at[k, pl.ds(pl.multiple_of(c * half, half), half)]
        who = (at(ze, xb), at(zf, x))[way]
        return pltpu.make_async_remote_copy(
            src_ref=s.at[who * per + k, pl.ds(pl.multiple_of(c * half, half), half)], dst_ref=dst,
            send_sem=t_send.at[way, k], recv_sem=t_recv.at[way, k],
            device_id=(dev(zm, xb), dev(zo, x))[way], device_id_type=MESH)

    def lend_on(k, way, core):
        ref = (across, along)[way].at[k, pl.ds(pl.multiple_of(core * half, half), half)]
        return pltpu.make_async_remote_copy(
            src_ref=ref, dst_ref=ref, send_sem=y_send.at[way, k], recv_sem=y_recv.at[way, k],
            device_id=twin, device_id_type=MESH)

    def back(k):
        ref = ef.at[pl.ds(k * tile, tile)]
        return pltpu.make_async_remote_copy(
            src_ref=ref, dst_ref=ref, send_sem=e_send.at[k], recv_sem=e_recv.at[k],
            device_id=dev(ze, x), device_id_type=MESH)

    def for_edge(k):
        def landed(mine, theirs):
            for kk, d in theirs:
                if kk == k:
                    pass_on(k, d).wait_recv()

        by_core(landed)
        if k < kept:
            for way in range(2):
                lend_on(k, way, 1 - c).wait_recv()
        turned = [(s.at[edge * per + k], r)]
        if k < kept:
            turned += [(across.at[k], at(zm, xb)), (along.at[k], at(zo, x))]
        accf[...] = jnp.zeros_like(accf)

        def rhs(q, b):
            return jnp.concatenate([ps[q][holder[b * per + j]] for j in range(per)], axis=0)

        for ref, b in turned:
            for q in range(spare):
                cs = pl.ds(q * wide, wide)
                accf[:, cs] += lax.dot_general(
                    ref[...], rhs(q, b), (((0,), (0,)), ((), ())), preferred_element_type=jnp.float32)

        def straight(d, carry):
            b = rel(d)
            lhs = ses[k][:, pl.ds(pl.multiple_of(b * rows, rows), rows)]
            for q in range(spare):
                cs = pl.ds(q * wide, wide)
                accf[:, cs] += jnp.dot(lhs, rhs(q, b), preferred_element_type=jnp.float32)
            return carry

        lax.fori_loop(3 if k < kept else 1, n, straight, 0)
        ef[pl.ds(k * tile, tile), :] = (-accf[...]).astype(ef.dtype)
        for q in range(spare):
            cs = pl.ds(q * wide, wide)
            term = ps[q][holder[edge * per + k]].astype(jnp.float32) * accf[:, cs]
            parts[r, :, cs] += jnp.sum(term, axis=0, keepdims=True)
        back(k).start()

    def middle():
        sent = []

        def go(copy):
            copy.start()
            sent.append(copy)

        ready = {}
        for k in range(per):
            last = max(turn(max(u for u, (kk, _) in enumerate(lst) if kk == k)) for lst in (same, other))
            ready.setdefault(max(last + 2, late + 3 + k, 4 + k), []).append(k)
        total = max(steps + 3, max(ready) + 1)
        waited = None
        for i in range(total):
            if i < steps:
                go(move(r, i, dev(zm, xb), 0, first(i)))
                go(move(r, i, dev(zo, x), 1, first(i)))
                if i >= late:
                    go(move(r, i, dev(ze, x), 2, first(i)))
            if i == 0:
                load_sigma()
            if i == 2:
                have_sigma()
            j = i - 1
            if 0 <= j < steps:
                b = at(ze, x)
                move(b, j, twin, 0).wait_recv()
                go(move(b, j, dev(zm, xb), 0))
                go(move(b, j, dev(zo, x), 1))
                b = at(zm, xb)
                move(b, j, twin, 0).wait_recv()
                go(move(b, j, dev(zo, x), 1))
                b = at(zo, x)
                move(b, j, twin, 0).wait_recv()
                if j >= late:
                    go(move(b, j, dev(ze, x), 2))
            j = i - 2
            if 0 <= j < steps:
                b = at(zf, x)
                move(b, j, twin, 0).wait_recv()
                go(move(b, j, dev(zm, xb), 0))
                if j >= late:
                    go(move(b, j, dev(ze, x), 2))
                move(at(ze, xb), j, twin, 0).wait_recv()
                move(at(zo, xb), j, twin, 0).wait_recv()
            k = i - 2
            if 0 <= k < kept:
                for way in range(2):
                    go(lend(k, way))
            k = i - 3
            if 0 <= k < kept:
                for way in range(2):
                    lend(k, way).wait_recv()
                    go(lend_on(k, way, c))
            j = i - 2

            def relay(mine, theirs):
                for u, (k, d) in enumerate(mine):
                    if turn(u) == j:
                        unit(k, d, twin).wait_recv()
                        pass_on(k, d).start()

            by_core(relay)
            j = i - 3
            if 0 <= j < steps:
                move(at(zf, xb), j, twin, 0).wait_recv()
                multiply(j)
                if j % split == split - 1:
                    q = j // split
                    finish(q, q - 2 if q >= 2 else None)
            for k in ready.get(i, ()):
                for_edge(k)

        for k in range(per):
            back(k).wait_send()

        def drained(mine, theirs):
            for k, d in mine:
                pass_on(k, d).wait_send()

        by_core(drained)
        for copy in sent:
            copy.wait_send()
        for q in range(max(chunks - 2, 0), chunks):
            put(q).wait()

    def end():
        sent = []

        def go(copy):
            copy.start()
            sent.append(copy)

        for i in range(steps + 4):
            if i < steps:
                go(move(r, i, dev(zm, x), 2, first(i)))
                if i >= late:
                    go(move(r, i, dev(ze, xb), 0, first(i)))

            def ship(mine, theirs):
                for u, (k, d) in enumerate(mine):
                    if turn(u) == i:
                        unit(k, d, dev(zm, x)).start()

            by_core(ship)
            if i == 0:
                load_sigma()
            if i == late:
                have_sigma()
            for lag, zz in ((1, zm), (2, zo), (3, zf)):
                j = i - lag
                if late <= j < steps:
                    b = at(zz, x)
                    move(b, j, twin, 0).wait_recv()
                    go(move(b, j, dev(ze, xb), 0))
            for lag, zz in ((1, ze), (2, zm), (3, zo), (4, zf)):
                j = i - lag
                if late <= j < steps:
                    move(at(zz, xb), j, twin, 0).wait_recv()
            j = i - 4
            if late <= j < steps:
                multiply(j)
                if j % split == split - 1:
                    q = j // split
                    finish(q, q - 2 if q - 2 >= spare else None)

        def home(k):
            where = pl.ds(k * tile, tile)
            return pltpu.make_async_copy(ef.at[where], out.at[where, pl.ds(0, spare * wide)], e_send.at[k])

        for k in range(per):
            back(k).wait_recv()
            home(k).start()
        for k in range(per):
            home(k).wait()

        def drained(mine, theirs):
            for k, d in mine:
                unit(k, d, dev(zm, x)).wait_send()

        by_core(drained)
        for copy in sent:
            copy.wait_send()
        for q in range(max(chunks - 2, spare), chunks):
            put(q).wait()

    @pl.when(z == zm)
    def _():
        middle()

    @pl.when(z == ze)
    def _():
        end()

    each(0, held, lambda j: far(j).wait_send())

    def share(k):
        return pltpu.make_async_remote_copy(
            src_ref=parts.at[r], dst_ref=parts.at[r], send_sem=v_send.at[k - 1], recv_sem=v_recv.at[k - 1],
            device_id=(g, lax.rem(r + k, n), c), device_id_type=MESH)

    def gone(k):
        frm = lax.rem(r + n - k, n)
        return pltpu.make_async_remote_copy(
            src_ref=parts.at[frm], dst_ref=parts.at[frm], send_sem=v_send.at[k - 1], recv_sem=v_recv.at[k - 1],
            device_id=(g, lax.rem(r + k, n), c), device_id_type=MESH)

    each(1, n, lambda k: share(k).start())
    each(1, n, lambda k: gone(k).wait_recv())
    each(1, n, lambda k: share(k).wait_send())
    total = parts[0]
    for k in range(1, n):
        total += parts[k]
    sums[...] = total


def plan(n, nc, per, tile, rows, cols):
    if n != 8 or nc != 2 or rows != per * tile:
        return None
    wide, split, spare, kept = 256, 2, 2, 3
    if cols % wide or cols // wide <= spare or per % split or kept > per or rows % nc:
        return None
    return wide, split, spare, kept


def body(n, nc, sigma_anc, panel, holder, dinv_diag):
    tiles = holder.shape[0]
    rows, width = sigma_anc.shape
    cols = panel.shape[1]
    per = tiles // n
    tile = panel.shape[0] // per
    fwd = (per + 1) // 2
    bwd = max(per - fwd, 1)
    ids = jnp.arange(tiles, dtype=jnp.int32)
    logical = jnp.sum(jnp.where(holder[:, None] == ids[None, :], ids[:, None], 0), axis=0, dtype=jnp.int32)
    dma = pltpu.SemaphoreType.DMA
    form = plan(n, nc, per, tile, rows, cols)
    if form is None:
        call = functools.partial(kernel, n, nc)
        limit = 60 << 20
        scratch = [
            pltpu.VMEM((width * nc // tile, rows, tile), sigma_anc.dtype),
            pltpu.VMEM((tiles, tile, cols), panel.dtype),
            pltpu.VMEM((rows, cols), jnp.float32),
            pltpu.VMEM((rows, cols), jnp.bfloat16),
            pltpu.VMEM((n, 1, cols), jnp.float32),
            dma,
            dma((2 * nc, width // tile)),
            dma((width // tile,)),
            dma((n * fwd,)),
            dma((n * fwd,)),
            dma((n * bwd,)),
            dma((n * bwd,)),
            dma((per,)),
            dma((n,)),
            dma((n,)),
        ]
    else:
        wide, split, spare, kept = form
        call = functools.partial(ladder, n, nc, *form)
        limit = 63 << 20
        chunks = cols // wide
        steps = chunks * split
        scratch = [
            pltpu.VMEM((width * nc // tile, rows, tile), sigma_anc.dtype),
            pltpu.VMEM((rows, wide), jnp.float32),
            pltpu.VMEM((2, rows, wide), jnp.bfloat16),
            pltpu.VMEM((rows, spare * wide), jnp.bfloat16),
            pltpu.VMEM((tile, spare * wide), jnp.float32),
            pltpu.VMEM((max(kept, 1), rows, tile), sigma_anc.dtype),
            pltpu.VMEM((max(kept, 1), rows, tile), sigma_anc.dtype),
            pltpu.VMEM((n, 1, cols), jnp.float32),
            dma((2, width // tile)),
            dma((width // tile,)),
            dma((chunks,)),
            dma((n, 3, steps)),
            dma((n, steps)),
            dma((per, n)),
            dma((per, n)),
            dma((per, n)),
            dma((per, n)),
            dma((2, max(kept, 1))),
            dma((2, max(kept, 1))),
            dma((2, max(kept, 1))),
            dma((2, max(kept, 1))),
            dma((per,)),
            dma((per,)),
            dma((chunks,)),
            dma((n,)),
            dma((n,)),
        ]
        scratch += [pltpu.VMEM((tiles, tile, wide), panel.dtype)] * chunks
        scratch += [pltpu.VMEM((tile, width * nc), sigma_anc.dtype)] * per
    out, sums = pl.pallas_call(
        call,
        out_shape=(
            jax.ShapeDtypeStruct((rows, cols), jnp.bfloat16),
            jax.ShapeDtypeStruct((1, cols), jnp.float32),
        ),
        in_specs=[
            pl.BlockSpec(memory_space=pltpu.SMEM),
            pl.BlockSpec(memory_space=pltpu.SMEM),
            pl.BlockSpec(memory_space=pl.ANY),
            pl.BlockSpec(memory_space=pl.ANY),
        ],
        out_specs=(
            pl.BlockSpec(memory_space=pl.ANY),
            pl.BlockSpec(memory_space=pltpu.VMEM),
        ),
        scratch_shapes=scratch,
        compiler_params=pltpu.CompilerParams(
            collective_id=0, has_side_effects=True, vmem_limit_bytes=limit
        ),
    )(holder, logical, sigma_anc, panel.reshape(per, tile, cols))
    return out, dinv_diag + sums.reshape(cols)


def solution(mesh):
    placed = (
        P(("groups", "row"), "col"),
        P(("groups", "row"), "col"),
        P("groups"),
        P(("groups", "col")),
    )
    return jax.shard_map(
        functools.partial(body, mesh.shape["row"], mesh.shape["col"]),
        mesh=mesh,
        in_specs=placed,
        out_specs=(P(("groups", "row"), "col"), P(("groups", "col"))),
        check_vma=False,
    )
```

```python
import functools

import jax
import jax.numpy as jnp
from jax import lax
from jax.experimental import pallas as pl
from jax.experimental.pallas import tpu as pltpu
from jax.sharding import PartitionSpec as P

MESH = pl.DeviceIdType.MESH


def block_of(size, most):
    block = min(size, most)
    while size % block:
        block -= 128
    return block


def kernel(n, nc, holder, logical, sigma, panel, out, sums, s, p, acc, staged, parts,
           own_sem, far_sem, near_sem, f_send, f_recv, b_send, b_recv, o_sem, v_send, v_recv):
    g = lax.axis_index("groups")
    r = lax.axis_index("row")
    c = lax.axis_index("col")
    per, tile, cols = panel.shape
    rows, width = sigma.shape
    tiles = p.shape[0]
    half = n // 2
    fwd = (per + 1) // 2
    bwd = per - fwd

    def row_of(at):
        at = lax.rem(at + 2 * n, n)
        odd = at // half
        return 2 * (at + odd * (2 * half - 1 - 2 * at)) + odd

    odd = lax.rem(r, 2)
    up = r // 2
    at = up + odd * (2 * half - 1 - 2 * up)
    after = (g, row_of(at + 1), c)
    before = (g, row_of(at - 1), c)

    barrier = pltpu.get_barrier_semaphore()

    def greet(k, carry):
        pl.semaphore_signal(barrier, 1, device_id=(g, lax.rem(r + k, n), c), device_id_type=MESH)
        return carry

    lax.fori_loop(1, n, greet, 0)
    for k in range(1, nc):
        pl.semaphore_signal(barrier, 1, device_id=(g, r, lax.rem(c + k, nc)), device_id_type=MESH)
    pl.semaphore_wait(barrier, n - 1 + nc - 1)

    def f_tile(k, i):
        return row_of(at - k) * per + i

    def b_tile(k, i):
        return row_of(at + k) * per + fwd + i

    def f_copy(k, i, src=None):
        t = f_tile(k, i)
        return pltpu.make_async_remote_copy(
            src_ref=p.at[t] if src is None else src, dst_ref=p.at[t],
            send_sem=f_send.at[k * fwd + i], recv_sem=f_recv.at[k * fwd + i],
            device_id=after, device_id_type=MESH)

    def b_copy(k, i, src=None):
        t = b_tile(k, i)
        return pltpu.make_async_remote_copy(
            src_ref=p.at[t] if src is None else src, dst_ref=p.at[t],
            send_sem=b_send.at[k * bwd + i], recv_sem=b_recv.at[k * bwd + i],
            device_id=before, device_id_type=MESH)

    def f_landed(k, i):
        t = f_tile(k, i)
        return pltpu.make_async_remote_copy(
            src_ref=p.at[t], dst_ref=p.at[t],
            send_sem=f_send.at[(k - 1) * fwd + i], recv_sem=f_recv.at[(k - 1) * fwd + i],
            device_id=after, device_id_type=MESH)

    def b_landed(k, i):
        t = b_tile(k, i)
        return pltpu.make_async_remote_copy(
            src_ref=p.at[t], dst_ref=p.at[t],
            send_sem=b_send.at[(k - 1) * bwd + i], recv_sem=b_recv.at[(k - 1) * bwd + i],
            device_id=before, device_id_type=MESH)

    for i in range(fwd):
        f_copy(0, i, panel.at[i]).start()
        if i < bwd:
            b_copy(0, i, panel.at[fwd + i]).start()

    held = width // tile

    def near(j):
        return pltpu.make_async_copy(
            sigma.at[:, pl.ds(pl.multiple_of(j * tile, tile), tile)], s.at[c * held + j], near_sem.at[j])

    def far(k, j):
        return pltpu.make_async_remote_copy(
            src_ref=sigma.at[:, pl.ds(pl.multiple_of(j * tile, tile), tile)], dst_ref=s.at[c * held + j],
            send_sem=far_sem.at[2 * k - 2, j], recv_sem=far_sem.at[2 * k - 1, j],
            device_id=(g, r, lax.rem(c + k, nc)), device_id_type=MESH)

    def far_landed(k, j):
        t = lax.rem(c + nc - k, nc) * held + j
        return pltpu.make_async_remote_copy(
            src_ref=s.at[t], dst_ref=s.at[t],
            send_sem=far_sem.at[2 * k - 2, j], recv_sem=far_sem.at[2 * k - 1, j],
            device_id=(g, r, lax.rem(c + k, nc)), device_id_type=MESH)

    def each(low, high, act):
        def step(k, carry):
            act(k)
            return carry
        lax.fori_loop(low, high, step, 0)

    for k in range(1, nc):
        each(0, held, lambda j: far(k, j).start())
    each(0, held, lambda j: near(j).start())
    own = pltpu.make_async_copy(panel, p.at[pl.ds(r * per, per)], own_sem)
    own.start()
    acc[...] = jnp.zeros_like(acc)
    own.wait()
    each(0, held, lambda j: near(j).wait())
    for k in range(1, nc):
        each(0, held, lambda j: far_landed(k, j).wait_recv())

    rb = block_of(rows, 512)
    cb = block_of(cols, 512)
    across = cols // cb

    def multiply(slots):
        columns = [logical[t] for t in slots]

        def block(q, carry):
            rs = pl.ds(pl.multiple_of((q // across) * rb, rb), rb)
            cs = pl.ds(pl.multiple_of(lax.rem(q, across) * cb, cb), cb)
            lhs = jnp.concatenate([s[w, rs, :] for w in columns], axis=1)
            rhs = jnp.concatenate([p[t, :, cs] for t in slots], axis=0)
            acc[rs, cs] += jnp.dot(lhs, rhs, preferred_element_type=jnp.float32)
            return carry

        lax.fori_loop(0, (rows // rb) * across, block, 0)

    def unit(u, carry):
        k = u // fwd
        i = lax.rem(u, fwd)

        @pl.when(k > 0)
        def _():
            f_landed(k, i).wait_recv()

            @pl.when(k < n - 1)
            def _():
                f_copy(k, i).start()

        if bwd == fwd:
            @pl.when(k > 0)
            def _():
                b_landed(k, i).wait_recv()

                @pl.when(k < n - 1)
                def _():
                    b_copy(k, i).start()

            multiply([f_tile(k, i), b_tile(k, i)])
        else:
            multiply([f_tile(k, i)])
            if bwd:
                @pl.when(i < bwd)
                def _():
                    @pl.when(k > 0)
                    def _():
                        b_landed(k, i).wait_recv()

                        @pl.when(k < n - 1)
                        def _():
                            b_copy(k, i).start()

                    multiply([b_tile(k, i)])
        return carry

    lax.fori_loop(0, n * fwd, unit, 0)

    parts[r] = jnp.zeros((1, cols), jnp.float32)

    def weigh(j, carry):
        where = pl.ds(pl.multiple_of(j * tile, tile), tile)
        mine = p[holder[r * per + j]]
        for b in range(across):
            cs = pl.ds(b * cb, cb)
            term = mine[:, b * cb:(b + 1) * cb].astype(jnp.float32) * acc[where, cs]
            parts[r, :, cs] += jnp.sum(term, axis=0, keepdims=True)
        return carry

    lax.fori_loop(0, per, weigh, 0)

    def share(k):
        to = lax.rem(r + k, n)
        return pltpu.make_async_remote_copy(
            src_ref=parts.at[r], dst_ref=parts.at[r],
            send_sem=v_send.at[k - 1], recv_sem=v_recv.at[k - 1],
            device_id=(g, to, c), device_id_type=MESH)

    def gone(k):
        frm = lax.rem(r + n - k, n)
        return pltpu.make_async_remote_copy(
            src_ref=parts.at[frm], dst_ref=parts.at[frm],
            send_sem=v_send.at[k - 1], recv_sem=v_recv.at[k - 1],
            device_id=(g, lax.rem(r + k, n), c), device_id_type=MESH)

    each(1, n, lambda k: share(k).start())

    def put(j):
        where = pl.ds(pl.multiple_of(j * tile, tile), tile)
        return pltpu.make_async_copy(staged.at[where], out.at[where], o_sem.at[j])

    def finish(j, carry):
        where = pl.ds(pl.multiple_of(j * tile, tile), tile)
        staged[where, :] = (-acc[where, :]).astype(staged.dtype)
        put(j).start()
        return carry

    lax.fori_loop(0, per, finish, 0)

    for k in range(1, nc):
        each(0, held, lambda j: far(k, j).wait_send())
    each(0, (n - 1) * fwd, lambda u: f_copy(u // fwd, lax.rem(u, fwd)).wait_send())
    if bwd:
        each(0, (n - 1) * bwd, lambda u: b_copy(u // bwd, lax.rem(u, bwd)).wait_send())
    each(0, per, lambda j: put(j).wait())
    each(1, n, lambda k: gone(k).wait_recv())
    each(1, n, lambda k: share(k).wait_send())
    total = parts[0]
    for k in range(1, n):
        total += parts[k]
    sums[...] = total


def ladder(n, nc, wide, table, fars, kept, lead, cap, stop, holder, logical, sigma, panel, out, sums,
           s, acc, staged, ef, accf, across, along, parts,
           far_sem, near_sem, own_sem, p_send, p_recv, u_send, u_recv, w_send, w_recv,
           t_send, t_recv, y_send, y_recv, e_send, e_recv, o_sem, v_send, v_recv, *bufs):
    g = lax.axis_index("groups")
    r = lax.axis_index("row")
    c = lax.axis_index("col")
    per, tile, cols = panel.shape
    rows, width = sigma.shape
    chunks = cols // wide
    ps, ses = bufs[:chunks], bufs[chunks:]
    held = width // tile
    steps = len(table)
    final = {q: i for i, (q, _, _) in enumerate(table)}
    near_edge = [i for i in range(steps) if table[i][0] not in fars]
    z = r // 2
    x = lax.rem(r, 2)
    xb = 1 - x
    side = z // 2
    ze, zm, zo, zf = 3 * side, 1 + side, 2 - side, 3 - 3 * side
    edge = 2 * ze + x

    def at(zz, xx):
        return 2 * zz + xx

    def dev(zz, xx):
        return (g, 2 * zz + xx, c)

    twin = (g, r, 1 - c)

    def own(q):
        return pltpu.make_async_copy(
            panel.at[:, :, pl.ds(q * wide, wide)], ps[q].at[pl.ds(r * per, per)], own_sem.at[q])

    for q in range(chunks):
        own(q).start()

    barrier = pltpu.get_barrier_semaphore()

    def greet(k, carry):
        pl.semaphore_signal(barrier, 1, device_id=(g, lax.rem(r + k, n), c), device_id_type=MESH)
        return carry

    lax.fori_loop(1, n, greet, 0)
    pl.semaphore_signal(barrier, 1, device_id=twin, device_id_type=MESH)
    pl.semaphore_wait(barrier, n)

    def each(low, high, act):
        def step(k, carry):
            act(k)
            return carry
        lax.fori_loop(low, high, step, 0)

    def piece(block, i):
        q, low, high = table[i]
        return ps[q].at[pl.ds(block * per + low, high - low)]

    def move(block, i, to, way):
        return pltpu.make_async_remote_copy(
            src_ref=piece(block, i), dst_ref=piece(block, i),
            send_sem=p_send.at[block, way, i], recv_sem=p_recv.at[block, i],
            device_id=to, device_id_type=MESH)

    def near(j):
        return pltpu.make_async_copy(
            sigma.at[:, pl.ds(pl.multiple_of(j * tile, tile), tile)], s.at[c * held + j], near_sem.at[j])

    def far(j):
        return pltpu.make_async_remote_copy(
            src_ref=sigma.at[:, pl.ds(pl.multiple_of(j * tile, tile), tile)], dst_ref=s.at[c * held + j],
            send_sem=far_sem.at[0, j], recv_sem=far_sem.at[1, j], device_id=twin, device_id_type=MESH)

    def far_landed(j):
        t = (1 - c) * held + j
        return pltpu.make_async_remote_copy(
            src_ref=s.at[t], dst_ref=s.at[t],
            send_sem=far_sem.at[0, j], recv_sem=far_sem.at[1, j], device_id=twin, device_id_type=MESH)

    def load_sigma():
        each(0, held, lambda j: far(j).start())
        each(0, held, lambda j: near(j).start())

    def have_sigma():
        each(0, held, lambda j: near(j).wait())
        each(0, held, lambda j: far_landed(j).wait_recv())
        parts[r] = jnp.zeros((1, cols), jnp.float32)

    rb = block_of(rows, 512)

    def multiply(i):
        q, low, high = table[i]
        if low == 0:
            acc[...] = jnp.zeros_like(acc)
        downs = rows // rb

        def block(u, carry):
            pair = u // downs
            rs = pl.ds(pl.multiple_of(lax.rem(u, downs) * rb, rb), rb)
            slots = [(2 * pair + m) * per + j for m in range(2) for j in range(low, high)]
            lhs = jnp.concatenate([s[logical[t], rs, :] for t in slots], axis=1)
            rhs = jnp.concatenate([ps[q][t] for t in slots], axis=0)
            acc[rs, :] += jnp.dot(lhs, rhs, preferred_element_type=jnp.float32)
            return carry

        lax.fori_loop(0, (n // 2) * downs, block, 0)

    def put(q, nth):
        return pltpu.make_async_copy(
            staged.at[nth % 2], out.at[:, pl.ds(q * wide, wide)], o_sem.at[q])

    def finish(q, mine):
        cs = pl.ds(q * wide, wide)
        nth = mine.index(q)
        if nth >= 2:
            put(mine[nth - 2], nth).wait()

        def weigh(j, carry):
            where = pl.ds(pl.multiple_of(j * tile, tile), tile)
            prod = acc[where, :]
            staged[nth % 2, where, :] = (-prod).astype(staged.dtype)
            term = ps[q][holder[r * per + j]].astype(jnp.float32) * prod
            parts[r, :, cs] += jnp.sum(term, axis=0, keepdims=True)
            return carry

        lax.fori_loop(0, per, weigh, 0)
        put(q, nth).start()

    def rel(idx):
        zz = idx // 2
        base = jnp.where(zz == 0, 1, jnp.where(zz == 1, 2, jnp.where(zz == 2, 0, 3)))
        return 2 * (base + side * (3 - 2 * base)) + lax.rem(x + idx, 2)

    units = [(k, d) for k in range(per) for d in range(1 if k >= kept else 3, n)]
    halves = units[0::2], units[1::2]

    def turn(u, group):
        return 1 + u * (steps - 1 - stop) // len(group)

    def strip(k, d):
        low = k if d == 4 else 0
        return pl.ds(rel(d) * per + low, per - low)

    def unit(k, d, to):
        return pltpu.make_async_remote_copy(
            src_ref=s.at[strip(k, d), pl.ds(k * tile, tile)], dst_ref=ses[k].at[strip(k, d)],
            send_sem=u_send.at[k, d], recv_sem=u_recv.at[k, d], device_id=to, device_id_type=MESH)

    def pass_on(k, d):
        ref = ses[k].at[strip(k, d)]
        return pltpu.make_async_remote_copy(
            src_ref=ref, dst_ref=ref, send_sem=w_send.at[k, d], recv_sem=w_recv.at[k, d],
            device_id=twin, device_id_type=MESH)

    def by_core(act):
        @pl.when(c == 0)
        def _():
            act(halves[0], halves[1])

        @pl.when(c != 0)
        def _():
            act(halves[1], halves[0])

    half = rows // nc

    def lend(k, way):
        dst = (across, along)[way].at[k, pl.ds(pl.multiple_of(c * half, half), half)]
        who = (at(ze, xb), at(zf, x))[way]
        return pltpu.make_async_remote_copy(
            src_ref=s.at[who * per + k, pl.ds(pl.multiple_of(c * half, half), half)], dst_ref=dst,
            send_sem=t_send.at[way, k], recv_sem=t_recv.at[way, k],
            device_id=(dev(zm, xb), dev(zo, x))[way], device_id_type=MESH)

    def lend_on(k, way, core):
        ref = (across, along)[way].at[k, pl.ds(pl.multiple_of(core * half, half), half)]
        return pltpu.make_async_remote_copy(
            src_ref=ref, dst_ref=ref, send_sem=y_send.at[way, k], recv_sem=y_recv.at[way, k],
            device_id=twin, device_id_type=MESH)

    def back(k, f):
        where = pl.ds(k * tile, tile)
        return pltpu.make_async_remote_copy(
            src_ref=ef.at[f, where], dst_ref=out.at[where, pl.ds(fars[f] * wide, wide)], send_sem=e_send.at[k, f], recv_sem=e_recv.at[k, f],
            device_id=dev(ze, x), device_id_type=MESH)

    def edge_landed(k):
        def landed(mine, theirs):
            for kk, d in theirs:
                if kk == k:
                    pass_on(k, d).wait_recv()

        by_core(landed)
        if k < kept:
            for way in range(2):
                lend_on(k, way, 1 - c).wait_recv()

    def for_edge(k, f):
        q = fars[f]

        def rhs(b):
            return jnp.concatenate([ps[q][holder[b * per + j]] for j in range(per)], axis=0)

        def turned(ref, b):
            return lax.dot_general(
                ref[...], rhs(b), (((0,), (0,)), ((), ())), preferred_element_type=jnp.float32)

        accf[...] = turned(s.at[edge * per + k], r)
        if k < kept:
            accf[...] += turned(across.at[k], at(zm, xb))
            accf[...] += turned(along.at[k], at(zo, x))

        def straight(d, carry):
            b = rel(d)
            lhs = jnp.concatenate([ses[k][b * per + j] for j in range(per)], axis=1)
            accf[...] += jnp.dot(lhs, rhs(b), preferred_element_type=jnp.float32)
            return carry

        lax.fori_loop(3 if k < kept else 1, 4, straight, 0)
        lax.fori_loop(5, n, straight, 0)
        lhs = jnp.concatenate(
            [ses[j][edge * per + k].T for j in range(k)] + [ses[k][edge * per + j] for j in range(k, per)], axis=1)
        accf[...] += jnp.dot(lhs, rhs(edge), preferred_element_type=jnp.float32)
        ef[f, pl.ds(k * tile, tile), :] = (-accf[...]).astype(ef.dtype)
        cs = pl.ds(q * wide, wide)
        term = ps[q][holder[edge * per + k]].astype(jnp.float32) * accf[...]
        parts[r, :, cs] += jnp.sum(term, axis=0, keepdims=True)
        back(k, f).start()

    def share(k):
        return pltpu.make_async_remote_copy(
            src_ref=parts.at[r], dst_ref=parts.at[r], send_sem=v_send.at[k - 1], recv_sem=v_recv.at[k - 1],
            device_id=(g, lax.rem(r + k, n), c), device_id_type=MESH)

    def gone(k):
        frm = lax.rem(r + n - k, n)
        return pltpu.make_async_remote_copy(
            src_ref=parts.at[frm], dst_ref=parts.at[frm], send_sem=v_send.at[k - 1], recv_sem=v_recv.at[k - 1],
            device_id=(g, lax.rem(r + k, n), c), device_id_type=MESH)

    def middle():
        sent = []

        def go(copy):
            copy.start()
            sent.append(copy)

        ready = {}
        fixed = []
        for k in range(per):
            last = max(turn(max(u for u, (kk, _) in enumerate(lst) if kk == k), lst) for lst in halves)
            fixed.append(max(last + 2, 5 + k if k < kept else 0))
        busy = {}
        for f, q in enumerate(fars):
            for k in range(per):
                i = max(fixed[k], final[q] + 3)
                while busy.get(i, 0) >= cap and i < steps + 1:
                    i += 1
                busy[i] = busy.get(i, 0) + 1
                ready.setdefault(i, []).append((k, f))
        fresh = set(range(per))
        total = max(steps + 2, max(ready) + 1)

        def give(i):
            if table[i][1] == 0:
                own(table[i][0]).wait()
            go(move(r, i, dev(zm, xb), 0))
            go(move(r, i, dev(zo, x), 1))
            if i in near_edge:
                go(move(r, i, dev(ze, x), 2))

        give(0)
        for i in range(total):
            if i + 1 < steps:
                give(i + 1)
            if i == 0:
                load_sigma()
            if i == 2:
                have_sigma()
            if i < steps:
                b = at(ze, x)
                move(b, i, twin, 0).wait_recv()
                go(move(b, i, dev(zm, xb), 0))
                go(move(b, i, dev(zo, x), 1))
                b = at(zm, xb)
                move(b, i, twin, 0).wait_recv()
                go(move(b, i, dev(zo, x), 1))
                b = at(zo, x)
                move(b, i, twin, 0).wait_recv()
                if i in near_edge:
                    go(move(b, i, dev(ze, x), 2))
            j = i - 1
            if 0 <= j < steps:
                b = at(zf, x)
                move(b, j, twin, 0).wait_recv()
                go(move(b, j, dev(zm, xb), 0))
                if j in near_edge:
                    go(move(b, j, dev(ze, x), 2))
                move(at(ze, xb), j, twin, 0).wait_recv()
                move(at(zo, xb), j, twin, 0).wait_recv()
            for k in range(kept):
                if i == 3 + k:
                    for way in range(2):
                        go(lend(k, way))
                if i == 4 + k:
                    for way in range(2):
                        lend(k, way).wait_recv()
                        go(lend_on(k, way, c))
            j = i - 2

            def relay(mine, theirs):
                for u, (k, d) in enumerate(mine):
                    if turn(u, mine) == j:
                        unit(k, d, twin).wait_recv()
                        pass_on(k, d).start()

            by_core(relay)
            for k, f in ready.get(i, ()):
                if k in fresh:
                    fresh.remove(k)
                    edge_landed(k)
                for_edge(k, f)
            j = i - 2
            if 0 <= j < steps:
                move(at(zf, xb), j, twin, 0).wait_recv()
                multiply(j)
                if final[table[j][0]] == j:
                    finish(table[j][0], list(range(chunks)))

        each(1, n, lambda k: share(k).start())
        for k in range(per):
            for f in range(len(fars)):
                back(k, f).wait_send()

        def drained(mine, theirs):
            for k, d in mine:
                pass_on(k, d).wait_send()

        by_core(drained)
        for copy in sent:
            copy.wait_send()
        for q in range(max(chunks - 2, 0), chunks):
            put(q, q).wait()

    def end():
        sent = []
        mine = [q for q in range(chunks) if q not in fars]

        def go(copy):
            copy.start()
            sent.append(copy)

        def give(i):
            if table[i][1] == 0:
                own(table[i][0]).wait()
            go(move(r, i, dev(zm, x), 2))
            if i in near_edge:
                go(move(r, i, dev(ze, xb), 0))

        for i in range(min(lead, steps)):
            give(i)
        for i in range(steps + 3):
            if i + lead < steps:
                give(i + lead)

            def ship(units, theirs):
                for u, (k, d) in enumerate(units):
                    if turn(u, units) == i:
                        unit(k, d, dev(zm, x)).start()

            if i == 0:
                load_sigma()
            if i == 1:
                have_sigma()
            by_core(ship)
            for lag, zz in ((0, zm), (1, zo), (2, zf)):
                j = i - lag
                if j in near_edge:
                    b = at(zz, x)
                    move(b, j, twin, 0).wait_recv()
                    go(move(b, j, dev(ze, xb), 0))
            for lag, zz in ((0, ze), (1, zm), (2, zo), (3, zf)):
                j = i - lag
                if j in near_edge:
                    move(at(zz, xb), j, twin, 0).wait_recv()
            j = i - 3
            if j in near_edge:
                multiply(j)
                if final[table[j][0]] == j:
                    finish(table[j][0], mine)

        each(1, n, lambda k: share(k).start())
        for k in range(per):
            for f in range(len(fars)):
                back(k, f).wait_recv()

        def drained(mine, theirs):
            for k, d in mine:
                unit(k, d, dev(zm, x)).wait_send()

        by_core(drained)
        for copy in sent:
            copy.wait_send()
        for nth in range(max(len(mine) - 2, 0), len(mine)):
            put(mine[nth], nth).wait()

    @pl.when(z == zm)
    def _():
        middle()

    @pl.when(z == ze)
    def _():
        end()

    each(0, held, lambda j: far(j).wait_send())

    each(1, n, lambda k: gone(k).wait_recv())
    each(1, n, lambda k: share(k).wait_send())
    total = parts[0]
    for k in range(1, n):
        total += parts[k]
    sums[...] = total


def plan(n, nc, per, tile, rows, cols):
    if n != 8 or nc != 2 or rows != per * tile:
        return None
    wide, fars, kept, lead, cap, stop = 256, (1, 3), 1, 2, 2, 0
    chunks = cols // wide
    if cols % wide or chunks <= max(fars) + 1 or per % 4 or kept > per or rows % nc:
        return None
    table = []
    for q in range(chunks):
        parts = 4 if q == chunks - 1 else 2
        table += [(q, h * per // parts, (h + 1) * per // parts) for h in range(parts)]
    return wide, tuple(table), fars, kept, lead, cap, stop


def body(n, nc, sigma_anc, panel, holder, dinv_diag):
    tiles = holder.shape[0]
    rows, width = sigma_anc.shape
    cols = panel.shape[1]
    per = tiles // n
    tile = panel.shape[0] // per
    fwd = (per + 1) // 2
    bwd = max(per - fwd, 1)
    ids = jnp.arange(tiles, dtype=jnp.int32)
    logical = jnp.sum(jnp.where(holder[:, None] == ids[None, :], ids[:, None], 0), axis=0, dtype=jnp.int32)
    dma = pltpu.SemaphoreType.DMA
    form = plan(n, nc, per, tile, rows, cols)
    if form is None:
        call = functools.partial(kernel, n, nc)
        limit = 60 << 20
        scratch = [
            pltpu.VMEM((width * nc // tile, rows, tile), sigma_anc.dtype),
            pltpu.VMEM((tiles, tile, cols), panel.dtype),
            pltpu.VMEM((rows, cols), jnp.float32),
            pltpu.VMEM((rows, cols), jnp.bfloat16),
            pltpu.VMEM((n, 1, cols), jnp.float32),
            dma,
            dma((2 * nc, width // tile)),
            dma((width // tile,)),
            dma((n * fwd,)),
            dma((n * fwd,)),
            dma((n * bwd,)),
            dma((n * bwd,)),
            dma((per,)),
            dma((n,)),
            dma((n,)),
        ]
    else:
        wide, table, fars, kept = form[:4]
        call = functools.partial(ladder, n, nc, *form)
        limit = 63 << 20
        chunks = cols // wide
        steps = len(table)
        scratch = [
            pltpu.VMEM((width * nc // tile, rows, tile), sigma_anc.dtype),
            pltpu.VMEM((rows, wide), jnp.float32),
            pltpu.VMEM((2, rows, wide), jnp.bfloat16),
            pltpu.VMEM((len(fars), rows, wide), jnp.bfloat16),
            pltpu.VMEM((tile, wide), jnp.float32),
            pltpu.VMEM((max(kept, 1), rows, tile), sigma_anc.dtype),
            pltpu.VMEM((max(kept, 1), rows, tile), sigma_anc.dtype),
            pltpu.VMEM((n, 1, cols), jnp.float32),
            dma((2, width // tile)),
            dma((width // tile,)),
            dma((chunks,)),
            dma((n, 3, steps)),
            dma((n, steps)),
            dma((per, n)),
            dma((per, n)),
            dma((per, n)),
            dma((per, n)),
            dma((2, max(kept, 1))),
            dma((2, max(kept, 1))),
            dma((2, max(kept, 1))),
            dma((2, max(kept, 1))),
            dma((per, len(fars))),
            dma((per, len(fars))),
            dma((chunks,)),
            dma((n,)),
            dma((n,)),
        ]
        scratch += [pltpu.VMEM((tiles, tile, wide), panel.dtype)] * chunks
        scratch += [pltpu.VMEM((tiles, tile, tile), sigma_anc.dtype)] * per
    out, sums = pl.pallas_call(
        call,
        out_shape=(
            jax.ShapeDtypeStruct((rows, cols), jnp.bfloat16),
            jax.ShapeDtypeStruct((1, cols), jnp.float32),
        ),
        in_specs=[
            pl.BlockSpec(memory_space=pltpu.SMEM),
            pl.BlockSpec(memory_space=pltpu.SMEM),
            pl.BlockSpec(memory_space=pl.ANY),
            pl.BlockSpec(memory_space=pl.ANY),
        ],
        out_specs=(
            pl.BlockSpec(memory_space=pl.ANY),
            pl.BlockSpec(memory_space=pltpu.VMEM),
        ),
        scratch_shapes=scratch,
        compiler_params=pltpu.CompilerParams(
            collective_id=0, has_side_effects=True, vmem_limit_bytes=limit
        ),
    )(holder, logical, sigma_anc, panel.reshape(per, tile, cols))
    return out, dinv_diag + sums.reshape(cols)


def solution(mesh):
    placed = (
        P(("groups", "row"), "col"),
        P(("groups", "row"), "col"),
        P("groups"),
        P(("groups", "col")),
    )
    return jax.shard_map(
        functools.partial(body, mesh.shape["row"], mesh.shape["col"]),
        mesh=mesh,
        in_specs=placed,
        out_specs=(P(("groups", "row"), "col"), P(("groups", "col"))),
        check_vma=False,
    )
```

```python
import functools

import jax
import jax.numpy as jnp
from jax import lax
from jax.experimental import pallas as pl
from jax.experimental.pallas import tpu as pltpu
from jax.sharding import PartitionSpec as P

MESH = pl.DeviceIdType.MESH


def block_of(size, most):
    block = min(size, most)
    while size % block:
        block -= 128
    return block


def kernel(n, nc, holder, logical, sigma, panel, out, sums, s, p, acc, staged, parts,
           own_sem, far_sem, near_sem, f_send, f_recv, b_send, b_recv, o_sem, v_send, v_recv):
    g = lax.axis_index("groups")
    r = lax.axis_index("row")
    c = lax.axis_index("col")
    per, tile, cols = panel.shape
    rows, width = sigma.shape
    tiles = p.shape[0]
    half = n // 2
    fwd = (per + 1) // 2
    bwd = per - fwd

    def row_of(at):
        at = lax.rem(at + 2 * n, n)
        odd = at // half
        return 2 * (at + odd * (2 * half - 1 - 2 * at)) + odd

    odd = lax.rem(r, 2)
    up = r // 2
    at = up + odd * (2 * half - 1 - 2 * up)
    after = (g, row_of(at + 1), c)
    before = (g, row_of(at - 1), c)

    barrier = pltpu.get_barrier_semaphore()

    def greet(k, carry):
        pl.semaphore_signal(barrier, 1, device_id=(g, lax.rem(r + k, n), c), device_id_type=MESH)
        return carry

    lax.fori_loop(1, n, greet, 0)
    for k in range(1, nc):
        pl.semaphore_signal(barrier, 1, device_id=(g, r, lax.rem(c + k, nc)), device_id_type=MESH)
    pl.semaphore_wait(barrier, n - 1 + nc - 1)

    def f_tile(k, i):
        return row_of(at - k) * per + i

    def b_tile(k, i):
        return row_of(at + k) * per + fwd + i

    def f_copy(k, i, src=None):
        t = f_tile(k, i)
        return pltpu.make_async_remote_copy(
            src_ref=p.at[t] if src is None else src, dst_ref=p.at[t],
            send_sem=f_send.at[k * fwd + i], recv_sem=f_recv.at[k * fwd + i],
            device_id=after, device_id_type=MESH)

    def b_copy(k, i, src=None):
        t = b_tile(k, i)
        return pltpu.make_async_remote_copy(
            src_ref=p.at[t] if src is None else src, dst_ref=p.at[t],
            send_sem=b_send.at[k * bwd + i], recv_sem=b_recv.at[k * bwd + i],
            device_id=before, device_id_type=MESH)

    def f_landed(k, i):
        t = f_tile(k, i)
        return pltpu.make_async_remote_copy(
            src_ref=p.at[t], dst_ref=p.at[t],
            send_sem=f_send.at[(k - 1) * fwd + i], recv_sem=f_recv.at[(k - 1) * fwd + i],
            device_id=after, device_id_type=MESH)

    def b_landed(k, i):
        t = b_tile(k, i)
        return pltpu.make_async_remote_copy(
            src_ref=p.at[t], dst_ref=p.at[t],
            send_sem=b_send.at[(k - 1) * bwd + i], recv_sem=b_recv.at[(k - 1) * bwd + i],
            device_id=before, device_id_type=MESH)

    for i in range(fwd):
        f_copy(0, i, panel.at[i]).start()
        if i < bwd:
            b_copy(0, i, panel.at[fwd + i]).start()

    held = width // tile

    def near(j):
        return pltpu.make_async_copy(
            sigma.at[:, pl.ds(pl.multiple_of(j * tile, tile), tile)], s.at[c * held + j], near_sem.at[j])

    def far(k, j):
        return pltpu.make_async_remote_copy(
            src_ref=sigma.at[:, pl.ds(pl.multiple_of(j * tile, tile), tile)], dst_ref=s.at[c * held + j],
            send_sem=far_sem.at[2 * k - 2, j], recv_sem=far_sem.at[2 * k - 1, j],
            device_id=(g, r, lax.rem(c + k, nc)), device_id_type=MESH)

    def far_landed(k, j):
        t = lax.rem(c + nc - k, nc) * held + j
        return pltpu.make_async_remote_copy(
            src_ref=s.at[t], dst_ref=s.at[t],
            send_sem=far_sem.at[2 * k - 2, j], recv_sem=far_sem.at[2 * k - 1, j],
            device_id=(g, r, lax.rem(c + k, nc)), device_id_type=MESH)

    def each(low, high, act):
        def step(k, carry):
            act(k)
            return carry
        lax.fori_loop(low, high, step, 0)

    for k in range(1, nc):
        each(0, held, lambda j: far(k, j).start())
    each(0, held, lambda j: near(j).start())
    own = pltpu.make_async_copy(panel, p.at[pl.ds(r * per, per)], own_sem)
    own.start()
    acc[...] = jnp.zeros_like(acc)
    own.wait()
    each(0, held, lambda j: near(j).wait())
    for k in range(1, nc):
        each(0, held, lambda j: far_landed(k, j).wait_recv())

    rb = block_of(rows, 512)
    cb = block_of(cols, 512)
    across = cols // cb

    def multiply(slots):
        columns = [logical[t] for t in slots]

        def block(q, carry):
            rs = pl.ds(pl.multiple_of((q // across) * rb, rb), rb)
            cs = pl.ds(pl.multiple_of(lax.rem(q, across) * cb, cb), cb)
            lhs = jnp.concatenate([s[w, rs, :] for w in columns], axis=1)
            rhs = jnp.concatenate([p[t, :, cs] for t in slots], axis=0)
            acc[rs, cs] += jnp.dot(lhs, rhs, preferred_element_type=jnp.float32)
            return carry

        lax.fori_loop(0, (rows // rb) * across, block, 0)

    def unit(u, carry):
        k = u // fwd
        i = lax.rem(u, fwd)

        @pl.when(k > 0)
        def _():
            f_landed(k, i).wait_recv()

            @pl.when(k < n - 1)
            def _():
                f_copy(k, i).start()

        if bwd == fwd:
            @pl.when(k > 0)
            def _():
                b_landed(k, i).wait_recv()

                @pl.when(k < n - 1)
                def _():
                    b_copy(k, i).start()

            multiply([f_tile(k, i), b_tile(k, i)])
        else:
            multiply([f_tile(k, i)])
            if bwd:
                @pl.when(i < bwd)
                def _():
                    @pl.when(k > 0)
                    def _():
                        b_landed(k, i).wait_recv()

                        @pl.when(k < n - 1)
                        def _():
                            b_copy(k, i).start()

                    multiply([b_tile(k, i)])
        return carry

    lax.fori_loop(0, n * fwd, unit, 0)

    parts[r] = jnp.zeros((1, cols), jnp.float32)

    def weigh(j, carry):
        where = pl.ds(pl.multiple_of(j * tile, tile), tile)
        mine = p[holder[r * per + j]]
        for b in range(across):
            cs = pl.ds(b * cb, cb)
            term = mine[:, b * cb:(b + 1) * cb].astype(jnp.float32) * acc[where, cs]
            parts[r, :, cs] += jnp.sum(term, axis=0, keepdims=True)
        return carry

    lax.fori_loop(0, per, weigh, 0)

    def share(k):
        to = lax.rem(r + k, n)
        return pltpu.make_async_remote_copy(
            src_ref=parts.at[r], dst_ref=parts.at[r],
            send_sem=v_send.at[k - 1], recv_sem=v_recv.at[k - 1],
            device_id=(g, to, c), device_id_type=MESH)

    def gone(k):
        frm = lax.rem(r + n - k, n)
        return pltpu.make_async_remote_copy(
            src_ref=parts.at[frm], dst_ref=parts.at[frm],
            send_sem=v_send.at[k - 1], recv_sem=v_recv.at[k - 1],
            device_id=(g, lax.rem(r + k, n), c), device_id_type=MESH)

    each(1, n, lambda k: share(k).start())

    def put(j):
        where = pl.ds(pl.multiple_of(j * tile, tile), tile)
        return pltpu.make_async_copy(staged.at[where], out.at[where], o_sem.at[j])

    def finish(j, carry):
        where = pl.ds(pl.multiple_of(j * tile, tile), tile)
        staged[where, :] = (-acc[where, :]).astype(staged.dtype)
        put(j).start()
        return carry

    lax.fori_loop(0, per, finish, 0)

    for k in range(1, nc):
        each(0, held, lambda j: far(k, j).wait_send())
    each(0, (n - 1) * fwd, lambda u: f_copy(u // fwd, lax.rem(u, fwd)).wait_send())
    if bwd:
        each(0, (n - 1) * bwd, lambda u: b_copy(u // bwd, lax.rem(u, bwd)).wait_send())
    each(0, per, lambda j: put(j).wait())
    each(1, n, lambda k: gone(k).wait_recv())
    each(1, n, lambda k: share(k).wait_send())
    total = parts[0]
    for k in range(1, n):
        total += parts[k]
    sums[...] = total


def ladder(n, nc, wide, table, fars, kept, lead, cap, stop, holder, logical, sigma, panel, out, sums,
           s, acc, staged, ef, accf, across, along, parts,
           far_sem, near_sem, own_sem, p_send, p_recv, u_send, u_recv, w_send, w_recv,
           t_send, t_recv, y_send, y_recv, e_send, e_recv, o_sem, v_send, v_recv, *bufs):
    g = lax.axis_index("groups")
    r = lax.axis_index("row")
    c = lax.axis_index("col")
    per, tile, cols = panel.shape
    rows, width = sigma.shape
    chunks = cols // wide
    ps, ses = bufs[:chunks], bufs[chunks:]
    held = width // tile
    steps = len(table)
    final = {q: i for i, (q, _, _) in enumerate(table)}
    near_edge = [i for i in range(steps) if table[i][0] not in fars]
    z = r // 2
    x = lax.rem(r, 2)
    xb = 1 - x
    side = z // 2
    ze, zm, zo, zf = 3 * side, 1 + side, 2 - side, 3 - 3 * side
    edge = 2 * ze + x

    def at(zz, xx):
        return 2 * zz + xx

    def dev(zz, xx):
        return (g, 2 * zz + xx, c)

    twin = (g, r, 1 - c)

    def own(q):
        return pltpu.make_async_copy(
            panel.at[:, :, pl.ds(q * wide, wide)], ps[q].at[pl.ds(r * per, per)], own_sem.at[q])

    for q in range(chunks):
        own(q).start()

    barrier = pltpu.get_barrier_semaphore()

    def greet(k, carry):
        pl.semaphore_signal(barrier, 1, device_id=(g, lax.rem(r + k, n), c), device_id_type=MESH)
        return carry

    lax.fori_loop(1, n, greet, 0)
    pl.semaphore_signal(barrier, 1, device_id=twin, device_id_type=MESH)
    pl.semaphore_wait(barrier, n)

    def each(low, high, act):
        def step(k, carry):
            act(k)
            return carry
        lax.fori_loop(low, high, step, 0)

    def piece(block, i):
        q, low, high = table[i]
        return ps[q].at[pl.ds(block * per + low, high - low)]

    def move(block, i, to, way):
        return pltpu.make_async_remote_copy(
            src_ref=piece(block, i), dst_ref=piece(block, i),
            send_sem=p_send.at[block, way, i], recv_sem=p_recv.at[block, i],
            device_id=to, device_id_type=MESH)

    def near(j):
        return pltpu.make_async_copy(
            sigma.at[:, pl.ds(pl.multiple_of(j * tile, tile), tile)], s.at[c * held + j], near_sem.at[j])

    def far(j):
        return pltpu.make_async_remote_copy(
            src_ref=sigma.at[:, pl.ds(pl.multiple_of(j * tile, tile), tile)], dst_ref=s.at[c * held + j],
            send_sem=far_sem.at[0, j], recv_sem=far_sem.at[1, j], device_id=twin, device_id_type=MESH)

    def far_landed(j):
        t = (1 - c) * held + j
        return pltpu.make_async_remote_copy(
            src_ref=s.at[t], dst_ref=s.at[t],
            send_sem=far_sem.at[0, j], recv_sem=far_sem.at[1, j], device_id=twin, device_id_type=MESH)

    def load_sigma():
        each(0, held, lambda j: far(j).start())
        each(0, held, lambda j: near(j).start())

    def have_sigma():
        each(0, held, lambda j: near(j).wait())
        each(0, held, lambda j: far_landed(j).wait_recv())
        parts[r] = jnp.zeros((1, cols), jnp.float32)

    rb = block_of(rows, 512)

    def multiply(i):
        q, low, high = table[i]
        if low == 0:
            acc[...] = jnp.zeros_like(acc)
        downs = rows // rb

        def block(u, carry):
            pair = u // downs
            rs = pl.ds(pl.multiple_of(lax.rem(u, downs) * rb, rb), rb)
            slots = [(2 * pair + m) * per + j for m in range(2) for j in range(low, high)]
            lhs = jnp.concatenate([s[logical[t], rs, :] for t in slots], axis=1)
            rhs = jnp.concatenate([ps[q][t] for t in slots], axis=0)
            acc[rs, :] += jnp.dot(lhs, rhs, preferred_element_type=jnp.float32)
            return carry

        lax.fori_loop(0, (n // 2) * downs, block, 0)

    def put(q, nth):
        return pltpu.make_async_copy(
            staged.at[nth % 2], out.at[:, pl.ds(q * wide, wide)], o_sem.at[q])

    def finish(q, mine):
        cs = pl.ds(q * wide, wide)
        nth = mine.index(q)
        if nth >= 2:
            put(mine[nth - 2], nth).wait()

        def weigh(j, carry):
            where = pl.ds(pl.multiple_of(j * tile, tile), tile)
            prod = acc[where, :]
            staged[nth % 2, where, :] = (-prod).astype(staged.dtype)
            term = ps[q][holder[r * per + j]].astype(jnp.float32) * prod
            parts[r, :, cs] += jnp.sum(term, axis=0, keepdims=True)
            return carry

        lax.fori_loop(0, per, weigh, 0)
        put(q, nth).start()

    def rel(idx):
        zz = idx // 2
        base = jnp.where(zz == 0, 1, jnp.where(zz == 1, 2, jnp.where(zz == 2, 0, 3)))
        return 2 * (base + side * (3 - 2 * base)) + lax.rem(x + idx, 2)

    units = [(k, d) for k in range(per) for d in range(1 if k >= kept else 3, n)]
    halves = units[0::2], units[1::2]

    def turn(u, group):
        return 1 + u * (steps - 1 - stop) // len(group)

    def strip(k, d):
        low = k if d == 4 else 0
        return pl.ds(rel(d) * per + low, per - low)

    def unit(k, d, to):
        return pltpu.make_async_remote_copy(
            src_ref=s.at[strip(k, d), pl.ds(k * tile, tile)], dst_ref=ses[k].at[strip(k, d)],
            send_sem=u_send.at[k, d], recv_sem=u_recv.at[k, d], device_id=to, device_id_type=MESH)

    def pass_on(k, d):
        ref = ses[k].at[strip(k, d)]
        return pltpu.make_async_remote_copy(
            src_ref=ref, dst_ref=ref, send_sem=w_send.at[k, d], recv_sem=w_recv.at[k, d],
            device_id=twin, device_id_type=MESH)

    def by_core(act):
        @pl.when(c == 0)
        def _():
            act(halves[0], halves[1])

        @pl.when(c != 0)
        def _():
            act(halves[1], halves[0])

    half = rows // nc

    def lend(k, way):
        dst = (across, along)[way].at[k, pl.ds(pl.multiple_of(c * half, half), half)]
        who = (at(ze, xb), at(zf, x))[way]
        return pltpu.make_async_remote_copy(
            src_ref=s.at[who * per + k, pl.ds(pl.multiple_of(c * half, half), half)], dst_ref=dst,
            send_sem=t_send.at[way, k], recv_sem=t_recv.at[way, k],
            device_id=(dev(zm, xb), dev(zo, x))[way], device_id_type=MESH)

    def lend_on(k, way, core):
        ref = (across, along)[way].at[k, pl.ds(pl.multiple_of(core * half, half), half)]
        return pltpu.make_async_remote_copy(
            src_ref=ref, dst_ref=ref, send_sem=y_send.at[way, k], recv_sem=y_recv.at[way, k],
            device_id=twin, device_id_type=MESH)

    def back(k, f):
        where = pl.ds(k * tile, tile)
        return pltpu.make_async_remote_copy(
            src_ref=ef.at[f, where], dst_ref=out.at[where, pl.ds(fars[f] * wide, wide)], send_sem=e_send.at[k, f], recv_sem=e_recv.at[k, f],
            device_id=dev(ze, x), device_id_type=MESH)

    def edge_landed(k):
        def landed(mine, theirs):
            for kk, d in theirs:
                if kk == k:
                    pass_on(k, d).wait_recv()

        by_core(landed)
        if k < kept:
            for way in range(2):
                lend_on(k, way, 1 - c).wait_recv()

    def for_edge(k, f):
        q = fars[f]

        def rhs(b):
            return jnp.concatenate([ps[q][holder[b * per + j]] for j in range(per)], axis=0)

        def turned(ref, b):
            return lax.dot_general(
                ref[...], rhs(b), (((0,), (0,)), ((), ())), preferred_element_type=jnp.float32)

        accf[...] = turned(s.at[edge * per + k], r)
        if k < kept:
            accf[...] += turned(across.at[k], at(zm, xb))
            accf[...] += turned(along.at[k], at(zo, x))

        def straight(d, carry):
            b = rel(d)
            lhs = jnp.concatenate([ses[k][b * per + j] for j in range(per)], axis=1)
            accf[...] += jnp.dot(lhs, rhs(b), preferred_element_type=jnp.float32)
            return carry

        lax.fori_loop(3 if k < kept else 1, 4, straight, 0)
        lax.fori_loop(5, n, straight, 0)
        lhs = jnp.concatenate(
            [ses[j][edge * per + k].T for j in range(k)] + [ses[k][edge * per + j] for j in range(k, per)], axis=1)
        accf[...] += jnp.dot(lhs, rhs(edge), preferred_element_type=jnp.float32)
        ef[f, pl.ds(k * tile, tile), :] = (-accf[...]).astype(ef.dtype)
        cs = pl.ds(q * wide, wide)
        term = ps[q][holder[edge * per + k]].astype(jnp.float32) * accf[...]
        parts[r, :, cs] += jnp.sum(term, axis=0, keepdims=True)
        back(k, f).start()

    def share(k):
        return pltpu.make_async_remote_copy(
            src_ref=parts.at[r], dst_ref=parts.at[r], send_sem=v_send.at[k - 1], recv_sem=v_recv.at[k - 1],
            device_id=(g, lax.rem(r + k, n), c), device_id_type=MESH)

    def gone(k):
        frm = lax.rem(r + n - k, n)
        return pltpu.make_async_remote_copy(
            src_ref=parts.at[frm], dst_ref=parts.at[frm], send_sem=v_send.at[k - 1], recv_sem=v_recv.at[k - 1],
            device_id=(g, lax.rem(r + k, n), c), device_id_type=MESH)

    def middle():
        sent = []

        def go(copy):
            copy.start()
            sent.append(copy)

        ready = {}
        fixed = []
        for k in range(per):
            last = max(turn(max(u for u, (kk, _) in enumerate(lst) if kk == k), lst) for lst in halves)
            fixed.append(max(last + 2, 5 + k if k < kept else 0))
        busy = {}
        for f, q in enumerate(fars):
            for k in range(per):
                i = max(fixed[k], final[q] + 3)
                while busy.get(i, 0) >= cap and i < steps + 1:
                    i += 1
                busy[i] = busy.get(i, 0) + 1
                ready.setdefault(i, []).append((k, f))
        fresh = set(range(per))
        total = max(steps + 2, max(ready) + 1)

        def give(i):
            if table[i][1] == 0:
                own(table[i][0]).wait()
            go(move(r, i, dev(zm, xb), 0))
            go(move(r, i, dev(zo, x), 1))
            if i in near_edge:
                go(move(r, i, dev(ze, x), 2))

        give(0)
        for i in range(total):
            if i + 1 < steps:
                give(i + 1)
            if i == 0:
                load_sigma()
            if i == 2:
                have_sigma()
            if i < steps:
                b = at(ze, x)
                move(b, i, twin, 0).wait_recv()
                go(move(b, i, dev(zm, xb), 0))
                go(move(b, i, dev(zo, x), 1))
                b = at(zm, xb)
                move(b, i, twin, 0).wait_recv()
                go(move(b, i, dev(zo, x), 1))
                b = at(zo, x)
                move(b, i, twin, 0).wait_recv()
                if i in near_edge:
                    go(move(b, i, dev(ze, x), 2))
            j = i - 1
            if 0 <= j < steps:
                b = at(zf, x)
                move(b, j, twin, 0).wait_recv()
                go(move(b, j, dev(zm, xb), 0))
                if j in near_edge:
                    go(move(b, j, dev(ze, x), 2))
                move(at(ze, xb), j, twin, 0).wait_recv()
                move(at(zo, xb), j, twin, 0).wait_recv()
            for k in range(kept):
                if i == 3 + k:
                    for way in range(2):
                        go(lend(k, way))
                if i == 4 + k:
                    for way in range(2):
                        lend(k, way).wait_recv()
                        go(lend_on(k, way, c))
            j = i - 2

            def relay(mine, theirs):
                for u, (k, d) in enumerate(mine):
                    if turn(u, mine) == j:
                        unit(k, d, twin).wait_recv()
                        pass_on(k, d).start()

            by_core(relay)
            for k, f in ready.get(i, ()):
                if k in fresh:
                    fresh.remove(k)
                    edge_landed(k)
                for_edge(k, f)
            j = i - 2
            if 0 <= j < steps:
                move(at(zf, xb), j, twin, 0).wait_recv()
                multiply(j)
                if final[table[j][0]] == j:
                    finish(table[j][0], list(range(chunks)))

        each(1, n, lambda k: share(k).start())
        for k in range(per):
            for f in range(len(fars)):
                back(k, f).wait_send()

        def drained(mine, theirs):
            for k, d in mine:
                pass_on(k, d).wait_send()

        by_core(drained)
        for copy in sent:
            copy.wait_send()
        for q in range(max(chunks - 2, 0), chunks):
            put(q, q).wait()

    def end():
        sent = []
        mine = [q for q in range(chunks) if q not in fars]

        def go(copy):
            copy.start()
            sent.append(copy)

        def give(i):
            if table[i][1] == 0:
                own(table[i][0]).wait()
            go(move(r, i, dev(zm, x), 2))
            if i in near_edge:
                go(move(r, i, dev(ze, xb), 0))

        for i in range(min(lead, steps)):
            give(i)
        for i in range(steps + 3):
            if i + lead < steps:
                give(i + lead)

            def ship(units, theirs):
                for u, (k, d) in enumerate(units):
                    if turn(u, units) == i:
                        unit(k, d, dev(zm, x)).start()

            if i == 0:
                load_sigma()
            if i == 1:
                have_sigma()
            by_core(ship)
            for lag, zz in ((0, zm), (1, zo), (2, zf)):
                j = i - lag
                if j in near_edge:
                    b = at(zz, x)
                    move(b, j, twin, 0).wait_recv()
                    go(move(b, j, dev(ze, xb), 0))
            for lag, zz in ((0, ze), (1, zm), (2, zo), (3, zf)):
                j = i - lag
                if j in near_edge:
                    move(at(zz, xb), j, twin, 0).wait_recv()
            j = i - 3
            if j in near_edge:
                multiply(j)
                if final[table[j][0]] == j:
                    finish(table[j][0], mine)

        each(1, n, lambda k: share(k).start())
        for k in range(per):
            for f in range(len(fars)):
                back(k, f).wait_recv()

        def drained(mine, theirs):
            for k, d in mine:
                unit(k, d, dev(zm, x)).wait_send()

        by_core(drained)
        for copy in sent:
            copy.wait_send()
        for nth in range(max(len(mine) - 2, 0), len(mine)):
            put(mine[nth], nth).wait()

    @pl.when(z == zm)
    def _():
        middle()

    @pl.when(z == ze)
    def _():
        end()

    each(0, held, lambda j: far(j).wait_send())

    each(1, n, lambda k: gone(k).wait_recv())
    each(1, n, lambda k: share(k).wait_send())
    total = parts[0]
    for k in range(1, n):
        total += parts[k]
    sums[...] = total


def plan(n, nc, per, tile, rows, cols):
    if n != 8 or nc != 2 or rows != per * tile:
        return None
    wide, fars, kept, lead, cap, stop = 256, (1, 3), 0, 2, 2, 0
    chunks = cols // wide
    if cols % wide or chunks <= max(fars) + 1 or per % 4 or kept > per or rows % nc:
        return None
    table = []
    for q in range(chunks):
        parts = 4 if q == chunks - 1 else 2
        table += [(q, h * per // parts, (h + 1) * per // parts) for h in range(parts)]
    return wide, tuple(table), fars, kept, lead, cap, stop


def body(n, nc, sigma_anc, panel, holder, dinv_diag):
    tiles = holder.shape[0]
    rows, width = sigma_anc.shape
    cols = panel.shape[1]
    per = tiles // n
    tile = panel.shape[0] // per
    fwd = (per + 1) // 2
    bwd = max(per - fwd, 1)
    ids = jnp.arange(tiles, dtype=jnp.int32)
    logical = jnp.sum(jnp.where(holder[:, None] == ids[None, :], ids[:, None], 0), axis=0, dtype=jnp.int32)
    dma = pltpu.SemaphoreType.DMA
    form = plan(n, nc, per, tile, rows, cols)
    if form is None:
        call = functools.partial(kernel, n, nc)
        limit = 60 << 20
        scratch = [
            pltpu.VMEM((width * nc // tile, rows, tile), sigma_anc.dtype),
            pltpu.VMEM((tiles, tile, cols), panel.dtype),
            pltpu.VMEM((rows, cols), jnp.float32),
            pltpu.VMEM((rows, cols), jnp.bfloat16),
            pltpu.VMEM((n, 1, cols), jnp.float32),
            dma,
            dma((2 * nc, width // tile)),
            dma((width // tile,)),
            dma((n * fwd,)),
            dma((n * fwd,)),
            dma((n * bwd,)),
            dma((n * bwd,)),
            dma((per,)),
            dma((n,)),
            dma((n,)),
        ]
    else:
        wide, table, fars, kept = form[:4]
        call = functools.partial(ladder, n, nc, *form)
        limit = 63 << 20
        chunks = cols // wide
        steps = len(table)
        scratch = [
            pltpu.VMEM((width * nc // tile, rows, tile), sigma_anc.dtype),
            pltpu.VMEM((rows, wide), jnp.float32),
            pltpu.VMEM((2, rows, wide), jnp.bfloat16),
            pltpu.VMEM((len(fars), rows, wide), jnp.bfloat16),
            pltpu.VMEM((tile, wide), jnp.float32),
            pltpu.VMEM((max(kept, 1), rows, tile), sigma_anc.dtype),
            pltpu.VMEM((max(kept, 1), rows, tile), sigma_anc.dtype),
            pltpu.VMEM((n, 1, cols), jnp.float32),
            dma((2, width // tile)),
            dma((width // tile,)),
            dma((chunks,)),
            dma((n, 3, steps)),
            dma((n, steps)),
            dma((per, n)),
            dma((per, n)),
            dma((per, n)),
            dma((per, n)),
            dma((2, max(kept, 1))),
            dma((2, max(kept, 1))),
            dma((2, max(kept, 1))),
            dma((2, max(kept, 1))),
            dma((per, len(fars))),
            dma((per, len(fars))),
            dma((chunks,)),
            dma((n,)),
            dma((n,)),
        ]
        scratch += [pltpu.VMEM((tiles, tile, wide), panel.dtype)] * chunks
        scratch += [pltpu.VMEM((tiles, tile, tile), sigma_anc.dtype)] * per
    out, sums = pl.pallas_call(
        call,
        out_shape=(
            jax.ShapeDtypeStruct((rows, cols), jnp.bfloat16),
            jax.ShapeDtypeStruct((1, cols), jnp.float32),
        ),
        in_specs=[
            pl.BlockSpec(memory_space=pltpu.SMEM),
            pl.BlockSpec(memory_space=pltpu.SMEM),
            pl.BlockSpec(memory_space=pl.ANY),
            pl.BlockSpec(memory_space=pl.ANY),
        ],
        out_specs=(
            pl.BlockSpec(memory_space=pl.ANY),
            pl.BlockSpec(memory_space=pltpu.VMEM),
        ),
        scratch_shapes=scratch,
        compiler_params=pltpu.CompilerParams(
            collective_id=0, has_side_effects=True, vmem_limit_bytes=limit
        ),
    )(holder, logical, sigma_anc, panel.reshape(per, tile, cols))
    return out, dinv_diag + sums.reshape(cols)


def solution(mesh):
    placed = (
        P(("groups", "row"), "col"),
        P(("groups", "row"), "col"),
        P("groups"),
        P(("groups", "col")),
    )
    return jax.shard_map(
        functools.partial(body, mesh.shape["row"], mesh.shape["col"]),
        mesh=mesh,
        in_specs=placed,
        out_specs=(P(("groups", "row"), "col"), P(("groups", "col"))),
        check_vma=False,
    )
```

```python
import functools

import jax
import jax.numpy as jnp
from jax import lax
from jax.experimental import pallas as pl
from jax.experimental.pallas import tpu as pltpu
from jax.sharding import PartitionSpec as P

MESH = pl.DeviceIdType.MESH


def block_of(size, most):
    block = min(size, most)
    while size % block:
        block -= 128
    return block


def kernel(n, nc, holder, logical, sigma, panel, out, sums, s, p, acc, staged, parts,
           own_sem, far_sem, near_sem, f_send, f_recv, b_send, b_recv, o_sem, v_send, v_recv):
    g = lax.axis_index("groups")
    r = lax.axis_index("row")
    c = lax.axis_index("col")
    per, tile, cols = panel.shape
    rows, width = sigma.shape
    tiles = p.shape[0]
    half = n // 2
    fwd = (per + 1) // 2
    bwd = per - fwd

    def row_of(at):
        at = lax.rem(at + 2 * n, n)
        odd = at // half
        return 2 * (at + odd * (2 * half - 1 - 2 * at)) + odd

    odd = lax.rem(r, 2)
    up = r // 2
    at = up + odd * (2 * half - 1 - 2 * up)
    after = (g, row_of(at + 1), c)
    before = (g, row_of(at - 1), c)

    barrier = pltpu.get_barrier_semaphore()

    def greet(k, carry):
        pl.semaphore_signal(barrier, 1, device_id=(g, lax.rem(r + k, n), c), device_id_type=MESH)
        return carry

    lax.fori_loop(1, n, greet, 0)
    for k in range(1, nc):
        pl.semaphore_signal(barrier, 1, device_id=(g, r, lax.rem(c + k, nc)), device_id_type=MESH)
    pl.semaphore_wait(barrier, n - 1 + nc - 1)

    def f_tile(k, i):
        return row_of(at - k) * per + i

    def b_tile(k, i):
        return row_of(at + k) * per + fwd + i

    def f_copy(k, i, src=None):
        t = f_tile(k, i)
        return pltpu.make_async_remote_copy(
            src_ref=p.at[t] if src is None else src, dst_ref=p.at[t],
            send_sem=f_send.at[k * fwd + i], recv_sem=f_recv.at[k * fwd + i],
            device_id=after, device_id_type=MESH)

    def b_copy(k, i, src=None):
        t = b_tile(k, i)
        return pltpu.make_async_remote_copy(
            src_ref=p.at[t] if src is None else src, dst_ref=p.at[t],
            send_sem=b_send.at[k * bwd + i], recv_sem=b_recv.at[k * bwd + i],
            device_id=before, device_id_type=MESH)

    def f_landed(k, i):
        t = f_tile(k, i)
        return pltpu.make_async_remote_copy(
            src_ref=p.at[t], dst_ref=p.at[t],
            send_sem=f_send.at[(k - 1) * fwd + i], recv_sem=f_recv.at[(k - 1) * fwd + i],
            device_id=after, device_id_type=MESH)

    def b_landed(k, i):
        t = b_tile(k, i)
        return pltpu.make_async_remote_copy(
            src_ref=p.at[t], dst_ref=p.at[t],
            send_sem=b_send.at[(k - 1) * bwd + i], recv_sem=b_recv.at[(k - 1) * bwd + i],
            device_id=before, device_id_type=MESH)

    for i in range(fwd):
        f_copy(0, i, panel.at[i]).start()
        if i < bwd:
            b_copy(0, i, panel.at[fwd + i]).start()

    held = width // tile

    def near(j):
        return pltpu.make_async_copy(
            sigma.at[:, pl.ds(pl.multiple_of(j * tile, tile), tile)], s.at[c * held + j], near_sem.at[j])

    def far(k, j):
        return pltpu.make_async_remote_copy(
            src_ref=sigma.at[:, pl.ds(pl.multiple_of(j * tile, tile), tile)], dst_ref=s.at[c * held + j],
            send_sem=far_sem.at[2 * k - 2, j], recv_sem=far_sem.at[2 * k - 1, j],
            device_id=(g, r, lax.rem(c + k, nc)), device_id_type=MESH)

    def far_landed(k, j):
        t = lax.rem(c + nc - k, nc) * held + j
        return pltpu.make_async_remote_copy(
            src_ref=s.at[t], dst_ref=s.at[t],
            send_sem=far_sem.at[2 * k - 2, j], recv_sem=far_sem.at[2 * k - 1, j],
            device_id=(g, r, lax.rem(c + k, nc)), device_id_type=MESH)

    def each(low, high, act):
        def step(k, carry):
            act(k)
            return carry
        lax.fori_loop(low, high, step, 0)

    for k in range(1, nc):
        each(0, held, lambda j: far(k, j).start())
    each(0, held, lambda j: near(j).start())
    own = pltpu.make_async_copy(panel, p.at[pl.ds(r * per, per)], own_sem)
    own.start()
    acc[...] = jnp.zeros_like(acc)
    own.wait()
    each(0, held, lambda j: near(j).wait())
    for k in range(1, nc):
        each(0, held, lambda j: far_landed(k, j).wait_recv())

    rb = block_of(rows, 512)
    cb = block_of(cols, 512)
    across = cols // cb

    def multiply(slots):
        columns = [logical[t] for t in slots]

        def block(q, carry):
            rs = pl.ds(pl.multiple_of((q // across) * rb, rb), rb)
            cs = pl.ds(pl.multiple_of(lax.rem(q, across) * cb, cb), cb)
            lhs = jnp.concatenate([s[w, rs, :] for w in columns], axis=1)
            rhs = jnp.concatenate([p[t, :, cs] for t in slots], axis=0)
            acc[rs, cs] += jnp.dot(lhs, rhs, preferred_element_type=jnp.float32)
            return carry

        lax.fori_loop(0, (rows // rb) * across, block, 0)

    def unit(u, carry):
        k = u // fwd
        i = lax.rem(u, fwd)

        @pl.when(k > 0)
        def _():
            f_landed(k, i).wait_recv()

            @pl.when(k < n - 1)
            def _():
                f_copy(k, i).start()

        if bwd == fwd:
            @pl.when(k > 0)
            def _():
                b_landed(k, i).wait_recv()

                @pl.when(k < n - 1)
                def _():
                    b_copy(k, i).start()

            multiply([f_tile(k, i), b_tile(k, i)])
        else:
            multiply([f_tile(k, i)])
            if bwd:
                @pl.when(i < bwd)
                def _():
                    @pl.when(k > 0)
                    def _():
                        b_landed(k, i).wait_recv()

                        @pl.when(k < n - 1)
                        def _():
                            b_copy(k, i).start()

                    multiply([b_tile(k, i)])
        return carry

    lax.fori_loop(0, n * fwd, unit, 0)

    parts[r] = jnp.zeros((1, cols), jnp.float32)

    def weigh(j, carry):
        where = pl.ds(pl.multiple_of(j * tile, tile), tile)
        mine = p[holder[r * per + j]]
        for b in range(across):
            cs = pl.ds(b * cb, cb)
            term = mine[:, b * cb:(b + 1) * cb].astype(jnp.float32) * acc[where, cs]
            parts[r, :, cs] += jnp.sum(term, axis=0, keepdims=True)
        return carry

    lax.fori_loop(0, per, weigh, 0)

    def share(k):
        to = lax.rem(r + k, n)
        return pltpu.make_async_remote_copy(
            src_ref=parts.at[r], dst_ref=parts.at[r],
            send_sem=v_send.at[k - 1], recv_sem=v_recv.at[k - 1],
            device_id=(g, to, c), device_id_type=MESH)

    def gone(k):
        frm = lax.rem(r + n - k, n)
        return pltpu.make_async_remote_copy(
            src_ref=parts.at[frm], dst_ref=parts.at[frm],
            send_sem=v_send.at[k - 1], recv_sem=v_recv.at[k - 1],
            device_id=(g, lax.rem(r + k, n), c), device_id_type=MESH)

    each(1, n, lambda k: share(k).start())

    def put(j):
        where = pl.ds(pl.multiple_of(j * tile, tile), tile)
        return pltpu.make_async_copy(staged.at[where], out.at[where], o_sem.at[j])

    def finish(j, carry):
        where = pl.ds(pl.multiple_of(j * tile, tile), tile)
        staged[where, :] = (-acc[where, :]).astype(staged.dtype)
        put(j).start()
        return carry

    lax.fori_loop(0, per, finish, 0)

    for k in range(1, nc):
        each(0, held, lambda j: far(k, j).wait_send())
    each(0, (n - 1) * fwd, lambda u: f_copy(u // fwd, lax.rem(u, fwd)).wait_send())
    if bwd:
        each(0, (n - 1) * bwd, lambda u: b_copy(u // bwd, lax.rem(u, bwd)).wait_send())
    each(0, per, lambda j: put(j).wait())
    each(1, n, lambda k: gone(k).wait_recv())
    each(1, n, lambda k: share(k).wait_send())
    total = parts[0]
    for k in range(1, n):
        total += parts[k]
    sums[...] = total


def ladder(n, nc, wide, table, fars, kept, lead, cap, stop, holder, logical, sigma, panel, out, sums,
           s, acc, staged, ef, accf, across, along, parts,
           far_sem, near_sem, own_sem, p_send, p_recv, u_send, u_recv, w_send, w_recv,
           t_send, t_recv, y_send, y_recv, e_send, e_recv, o_sem, v_send, v_recv, *bufs):
    g = lax.axis_index("groups")
    r = lax.axis_index("row")
    c = lax.axis_index("col")
    per, tile, cols = panel.shape
    rows, width = sigma.shape
    chunks = cols // wide
    ps, ses = bufs[:chunks], bufs[chunks:]
    held = width // tile
    steps = len(table)
    final = {q: i for i, (q, _, _) in enumerate(table)}
    near_edge = [i for i in range(steps) if table[i][0] not in fars]
    z = r // 2
    x = lax.rem(r, 2)
    xb = 1 - x
    side = z // 2
    ze, zm, zo, zf = 3 * side, 1 + side, 2 - side, 3 - 3 * side
    edge = 2 * ze + x

    def at(zz, xx):
        return 2 * zz + xx

    def dev(zz, xx):
        return (g, 2 * zz + xx, c)

    twin = (g, r, 1 - c)

    def own(q):
        return pltpu.make_async_copy(
            panel.at[:, :, pl.ds(q * wide, wide)], ps[q].at[pl.ds(r * per, per)], own_sem.at[q])

    for q in range(chunks):
        own(q).start()

    barrier = pltpu.get_barrier_semaphore()

    def greet(k, carry):
        pl.semaphore_signal(barrier, 1, device_id=(g, lax.rem(r + k, n), c), device_id_type=MESH)
        return carry

    lax.fori_loop(1, n, greet, 0)
    pl.semaphore_signal(barrier, 1, device_id=twin, device_id_type=MESH)
    pl.semaphore_wait(barrier, n)

    def each(low, high, act):
        def step(k, carry):
            act(k)
            return carry
        lax.fori_loop(low, high, step, 0)

    def piece(block, i):
        q, low, high = table[i]
        return ps[q].at[pl.ds(block * per + low, high - low)]

    def move(block, i, to, way):
        return pltpu.make_async_remote_copy(
            src_ref=piece(block, i), dst_ref=piece(block, i),
            send_sem=p_send.at[block, way, i], recv_sem=p_recv.at[block, i],
            device_id=to, device_id_type=MESH)

    def near(j):
        return pltpu.make_async_copy(
            sigma.at[:, pl.ds(pl.multiple_of(j * tile, tile), tile)], s.at[c * held + j], near_sem.at[j])

    def far(j):
        return pltpu.make_async_remote_copy(
            src_ref=sigma.at[:, pl.ds(pl.multiple_of(j * tile, tile), tile)], dst_ref=s.at[c * held + j],
            send_sem=far_sem.at[0, j], recv_sem=far_sem.at[1, j], device_id=twin, device_id_type=MESH)

    def far_landed(j):
        t = (1 - c) * held + j
        return pltpu.make_async_remote_copy(
            src_ref=s.at[t], dst_ref=s.at[t],
            send_sem=far_sem.at[0, j], recv_sem=far_sem.at[1, j], device_id=twin, device_id_type=MESH)

    def load_sigma():
        each(0, held, lambda j: far(j).start())
        each(0, held, lambda j: near(j).start())

    def have_sigma():
        each(0, held, lambda j: near(j).wait())
        each(0, held, lambda j: far_landed(j).wait_recv())
        parts[r] = jnp.zeros((1, cols), jnp.float32)

    rb = block_of(rows, 512)

    def multiply(i):
        q, low, high = table[i]
        if low == 0:
            acc[...] = jnp.zeros_like(acc)
        downs = rows // rb

        def block(u, carry):
            pair = u // downs
            rs = pl.ds(pl.multiple_of(lax.rem(u, downs) * rb, rb), rb)
            slots = [(2 * pair + m) * per + j for m in range(2) for j in range(low, high)]
            lhs = jnp.concatenate([s[logical[t], rs, :] for t in slots], axis=1)
            rhs = jnp.concatenate([ps[q][t] for t in slots], axis=0)
            acc[rs, :] += jnp.dot(lhs, rhs, preferred_element_type=jnp.float32)
            return carry

        lax.fori_loop(0, (n // 2) * downs, block, 0)

    def put(q, nth):
        return pltpu.make_async_copy(
            staged.at[nth % 2], out.at[:, pl.ds(q * wide, wide)], o_sem.at[q])

    def finish(q, mine):
        cs = pl.ds(q * wide, wide)
        nth = mine.index(q)
        if nth >= 2:
            put(mine[nth - 2], nth).wait()

        def weigh(j, carry):
            where = pl.ds(pl.multiple_of(j * tile, tile), tile)
            prod = acc[where, :]
            staged[nth % 2, where, :] = (-prod).astype(staged.dtype)
            term = ps[q][holder[r * per + j]].astype(jnp.float32) * prod
            parts[r, :, cs] += jnp.sum(term, axis=0, keepdims=True)
            return carry

        lax.fori_loop(0, per, weigh, 0)
        put(q, nth).start()

    def rel(idx):
        zz = idx // 2
        base = jnp.where(zz == 0, 1, jnp.where(zz == 1, 2, jnp.where(zz == 2, 0, 3)))
        return 2 * (base + side * (3 - 2 * base)) + lax.rem(x + idx, 2)

    units = [(k, d) for k in range(per) for d in range(1 if k >= kept else 3, n)]
    halves = units[0::2], units[1::2]

    def turn(u, group):
        return 1 + u * (steps - 1 - stop) // len(group)

    def strip(k, d):
        low = k if d == 4 else 0
        return pl.ds(rel(d) * per + low, per - low)

    def unit(k, d, to):
        return pltpu.make_async_remote_copy(
            src_ref=s.at[strip(k, d), pl.ds(k * tile, tile)], dst_ref=ses[k].at[strip(k, d)],
            send_sem=u_send.at[k, d], recv_sem=u_recv.at[k, d], device_id=to, device_id_type=MESH)

    def pass_on(k, d):
        ref = ses[k].at[strip(k, d)]
        return pltpu.make_async_remote_copy(
            src_ref=ref, dst_ref=ref, send_sem=w_send.at[k, d], recv_sem=w_recv.at[k, d],
            device_id=twin, device_id_type=MESH)

    def by_core(act):
        @pl.when(c == 0)
        def _():
            act(halves[0], halves[1])

        @pl.when(c != 0)
        def _():
            act(halves[1], halves[0])

    half = rows // nc

    def lend(k, way):
        dst = (across, along)[way].at[k, pl.ds(pl.multiple_of(c * half, half), half)]
        who = (at(ze, xb), at(zf, x))[way]
        return pltpu.make_async_remote_copy(
            src_ref=s.at[who * per + k, pl.ds(pl.multiple_of(c * half, half), half)], dst_ref=dst,
            send_sem=t_send.at[way, k], recv_sem=t_recv.at[way, k],
            device_id=(dev(zm, xb), dev(zo, x))[way], device_id_type=MESH)

    def lend_on(k, way, core):
        ref = (across, along)[way].at[k, pl.ds(pl.multiple_of(core * half, half), half)]
        return pltpu.make_async_remote_copy(
            src_ref=ref, dst_ref=ref, send_sem=y_send.at[way, k], recv_sem=y_recv.at[way, k],
            device_id=twin, device_id_type=MESH)

    def back(k, f):
        where = pl.ds(k * tile, tile)
        return pltpu.make_async_remote_copy(
            src_ref=ef.at[f, where], dst_ref=out.at[where, pl.ds(fars[f] * wide, wide)], send_sem=e_send.at[k, f], recv_sem=e_recv.at[k, f],
            device_id=dev(ze, x), device_id_type=MESH)

    def edge_landed(k):
        def landed(mine, theirs):
            for kk, d in theirs:
                if kk == k:
                    pass_on(k, d).wait_recv()

        by_core(landed)
        if k < kept:
            for way in range(2):
                lend_on(k, way, 1 - c).wait_recv()

    def for_edge(k, f):
        q = fars[f]

        def rhs(b):
            return jnp.concatenate([ps[q][holder[b * per + j]] for j in range(per)], axis=0)

        def turned(ref, b):
            return lax.dot_general(
                ref[...], rhs(b), (((0,), (0,)), ((), ())), preferred_element_type=jnp.float32)

        accf[...] = turned(s.at[edge * per + k], r)
        if k < kept:
            accf[...] += turned(across.at[k], at(zm, xb))
            accf[...] += turned(along.at[k], at(zo, x))

        def straight(d, carry):
            b = rel(d)
            lhs = jnp.concatenate([ses[k][b * per + j] for j in range(per)], axis=1)
            accf[...] += jnp.dot(lhs, rhs(b), preferred_element_type=jnp.float32)
            return carry

        lax.fori_loop(3 if k < kept else 1, 4, straight, 0)
        lax.fori_loop(5, n, straight, 0)
        lhs = jnp.concatenate(
            [ses[j][edge * per + k].T for j in range(k)] + [ses[k][edge * per + j] for j in range(k, per)], axis=1)
        accf[...] += jnp.dot(lhs, rhs(edge), preferred_element_type=jnp.float32)
        ef[f, pl.ds(k * tile, tile), :] = (-accf[...]).astype(ef.dtype)
        cs = pl.ds(q * wide, wide)
        term = ps[q][holder[edge * per + k]].astype(jnp.float32) * accf[...]
        parts[r, :, cs] += jnp.sum(term, axis=0, keepdims=True)
        back(k, f).start()

    def share(k):
        return pltpu.make_async_remote_copy(
            src_ref=parts.at[r], dst_ref=parts.at[r], send_sem=v_send.at[k - 1], recv_sem=v_recv.at[k - 1],
            device_id=(g, lax.rem(r + k, n), c), device_id_type=MESH)

    def gone(k):
        frm = lax.rem(r + n - k, n)
        return pltpu.make_async_remote_copy(
            src_ref=parts.at[frm], dst_ref=parts.at[frm], send_sem=v_send.at[k - 1], recv_sem=v_recv.at[k - 1],
            device_id=(g, lax.rem(r + k, n), c), device_id_type=MESH)

    def middle():
        sent = []

        def go(copy):
            copy.start()
            sent.append(copy)

        ready = {}
        fixed = []
        for k in range(per):
            last = max(turn(max(u for u, (kk, _) in enumerate(lst) if kk == k), lst) for lst in halves)
            fixed.append(max(last + 2, 5 + k if k < kept else 0))
        busy = {}
        for f, q in enumerate(fars):
            for k in range(per):
                i = max(fixed[k], final[q] + 3)
                while busy.get(i, 0) >= cap and i < steps + 1:
                    i += 1
                busy[i] = busy.get(i, 0) + 1
                ready.setdefault(i, []).append((k, f))
        fresh = set(range(per))
        total = max(steps + 2, max(ready) + 1)

        def give(i):
            if table[i][1] == 0:
                own(table[i][0]).wait()
            go(move(r, i, dev(zm, xb), 0))
            go(move(r, i, dev(zo, x), 1))
            if i in near_edge:
                go(move(r, i, dev(ze, x), 2))

        give(0)
        for i in range(total):
            if i + 1 < steps:
                give(i + 1)
            if i == 0:
                load_sigma()
            if i == 2:
                have_sigma()
            if i < steps:
                b = at(ze, x)
                move(b, i, twin, 0).wait_recv()
                go(move(b, i, dev(zm, xb), 0))
                go(move(b, i, dev(zo, x), 1))
                b = at(zm, xb)
                move(b, i, twin, 0).wait_recv()
                go(move(b, i, dev(zo, x), 1))
                b = at(zo, x)
                move(b, i, twin, 0).wait_recv()
                if i in near_edge:
                    go(move(b, i, dev(ze, x), 2))
            j = i - 1
            if 0 <= j < steps:
                b = at(zf, x)
                move(b, j, twin, 0).wait_recv()
                go(move(b, j, dev(zm, xb), 0))
                if j in near_edge:
                    go(move(b, j, dev(ze, x), 2))
                move(at(ze, xb), j, twin, 0).wait_recv()
                move(at(zo, xb), j, twin, 0).wait_recv()
            for k in range(kept):
                if i == 3 + k:
                    for way in range(2):
                        go(lend(k, way))
                if i == 4 + k:
                    for way in range(2):
                        lend(k, way).wait_recv()
                        go(lend_on(k, way, c))
            j = i - 2

            def relay(mine, theirs):
                for u, (k, d) in enumerate(mine):
                    if turn(u, mine) == j:
                        unit(k, d, twin).wait_recv()
                        pass_on(k, d).start()

            by_core(relay)
            for k, f in ready.get(i, ()):
                if k in fresh:
                    fresh.remove(k)
                    edge_landed(k)
                for_edge(k, f)
            j = i - 2
            if 0 <= j < steps:
                move(at(zf, xb), j, twin, 0).wait_recv()
                multiply(j)
                if final[table[j][0]] == j:
                    finish(table[j][0], list(range(chunks)))

        each(1, n, lambda k: share(k).start())
        for k in range(per):
            for f in range(len(fars)):
                back(k, f).wait_send()

        def drained(mine, theirs):
            for k, d in mine:
                pass_on(k, d).wait_send()

        by_core(drained)
        for copy in sent:
            copy.wait_send()
        for q in range(max(chunks - 2, 0), chunks):
            put(q, q).wait()

    def end():
        sent = []
        mine = [q for q in range(chunks) if q not in fars]

        def go(copy):
            copy.start()
            sent.append(copy)

        def give(i):
            if table[i][1] == 0:
                own(table[i][0]).wait()
            go(move(r, i, dev(zm, x), 2))
            if i in near_edge:
                go(move(r, i, dev(ze, xb), 0))

        for i in range(min(lead, steps)):
            give(i)
        for i in range(steps + 3):
            if i + lead < steps:
                give(i + lead)

            def ship(units, theirs):
                for u, (k, d) in enumerate(units):
                    if turn(u, units) == i:
                        unit(k, d, dev(zm, x)).start()

            if i == 0:
                load_sigma()
            if i == 1:
                have_sigma()
            by_core(ship)
            for lag, zz in ((0, zm), (1, zo), (2, zf)):
                j = i - lag
                if j in near_edge:
                    b = at(zz, x)
                    move(b, j, twin, 0).wait_recv()
                    go(move(b, j, dev(ze, xb), 0))
            for lag, zz in ((0, ze), (1, zm), (2, zo), (3, zf)):
                j = i - lag
                if j in near_edge:
                    move(at(zz, xb), j, twin, 0).wait_recv()
            j = i - 3
            if j in near_edge:
                multiply(j)
                if final[table[j][0]] == j:
                    finish(table[j][0], mine)

        each(1, n, lambda k: share(k).start())
        for k in range(per):
            for f in range(len(fars)):
                back(k, f).wait_recv()

        def drained(mine, theirs):
            for k, d in mine:
                unit(k, d, dev(zm, x)).wait_send()

        by_core(drained)
        for copy in sent:
            copy.wait_send()
        for nth in range(max(len(mine) - 2, 0), len(mine)):
            put(mine[nth], nth).wait()

    @pl.when(z == zm)
    def _():
        middle()

    @pl.when(z == ze)
    def _():
        end()

    each(0, held, lambda j: far(j).wait_send())

    each(1, n, lambda k: gone(k).wait_recv())
    each(1, n, lambda k: share(k).wait_send())
    total = parts[0]
    for k in range(1, n):
        total += parts[k]
    sums[...] = total


def plan(n, nc, per, tile, rows, cols):
    if n != 8 or nc != 2 or rows != per * tile:
        return None
    wide, fars, kept, lead, cap, stop = 256, (0, 3), 0, 2, 2, 0
    chunks = cols // wide
    if cols % wide or chunks <= max(fars) + 1 or per % 4 or kept > per or rows % nc:
        return None
    table = []
    for q in range(chunks):
        parts = 4 if q == chunks - 1 else 2
        table += [(q, h * per // parts, (h + 1) * per // parts) for h in range(parts)]
    return wide, tuple(table), fars, kept, lead, cap, stop


def body(n, nc, sigma_anc, panel, holder, dinv_diag):
    tiles = holder.shape[0]
    rows, width = sigma_anc.shape
    cols = panel.shape[1]
    per = tiles // n
    tile = panel.shape[0] // per
    fwd = (per + 1) // 2
    bwd = max(per - fwd, 1)
    ids = jnp.arange(tiles, dtype=jnp.int32)
    logical = jnp.sum(jnp.where(holder[:, None] == ids[None, :], ids[:, None], 0), axis=0, dtype=jnp.int32)
    dma = pltpu.SemaphoreType.DMA
    form = plan(n, nc, per, tile, rows, cols)
    if form is None:
        call = functools.partial(kernel, n, nc)
        limit = 60 << 20
        scratch = [
            pltpu.VMEM((width * nc // tile, rows, tile), sigma_anc.dtype),
            pltpu.VMEM((tiles, tile, cols), panel.dtype),
            pltpu.VMEM((rows, cols), jnp.float32),
            pltpu.VMEM((rows, cols), jnp.bfloat16),
            pltpu.VMEM((n, 1, cols), jnp.float32),
            dma,
            dma((2 * nc, width // tile)),
            dma((width // tile,)),
            dma((n * fwd,)),
            dma((n * fwd,)),
            dma((n * bwd,)),
            dma((n * bwd,)),
            dma((per,)),
            dma((n,)),
            dma((n,)),
        ]
    else:
        wide, table, fars, kept = form[:4]
        call = functools.partial(ladder, n, nc, *form)
        limit = 63 << 20
        chunks = cols // wide
        steps = len(table)
        scratch = [
            pltpu.VMEM((width * nc // tile, rows, tile), sigma_anc.dtype),
            pltpu.VMEM((rows, wide), jnp.float32),
            pltpu.VMEM((2, rows, wide), jnp.bfloat16),
            pltpu.VMEM((len(fars), rows, wide), jnp.bfloat16),
            pltpu.VMEM((tile, wide), jnp.float32),
            pltpu.VMEM((max(kept, 1), rows, tile), sigma_anc.dtype),
            pltpu.VMEM((max(kept, 1), rows, tile), sigma_anc.dtype),
            pltpu.VMEM((n, 1, cols), jnp.float32),
            dma((2, width // tile)),
            dma((width // tile,)),
            dma((chunks,)),
            dma((n, 3, steps)),
            dma((n, steps)),
            dma((per, n)),
            dma((per, n)),
            dma((per, n)),
            dma((per, n)),
            dma((2, max(kept, 1))),
            dma((2, max(kept, 1))),
            dma((2, max(kept, 1))),
            dma((2, max(kept, 1))),
            dma((per, len(fars))),
            dma((per, len(fars))),
            dma((chunks,)),
            dma((n,)),
            dma((n,)),
        ]
        scratch += [pltpu.VMEM((tiles, tile, wide), panel.dtype)] * chunks
        scratch += [pltpu.VMEM((tiles, tile, tile), sigma_anc.dtype)] * per
    out, sums = pl.pallas_call(
        call,
        out_shape=(
            jax.ShapeDtypeStruct((rows, cols), jnp.bfloat16),
            jax.ShapeDtypeStruct((1, cols), jnp.float32),
        ),
        in_specs=[
            pl.BlockSpec(memory_space=pltpu.SMEM),
            pl.BlockSpec(memory_space=pltpu.SMEM),
            pl.BlockSpec(memory_space=pl.ANY),
            pl.BlockSpec(memory_space=pl.ANY),
        ],
        out_specs=(
            pl.BlockSpec(memory_space=pl.ANY),
            pl.BlockSpec(memory_space=pltpu.VMEM),
        ),
        scratch_shapes=scratch,
        compiler_params=pltpu.CompilerParams(
            collective_id=0, has_side_effects=True, vmem_limit_bytes=limit
        ),
    )(holder, logical, sigma_anc, panel.reshape(per, tile, cols))
    return out, dinv_diag + sums.reshape(cols)


def solution(mesh):
    placed = (
        P(("groups", "row"), "col"),
        P(("groups", "row"), "col"),
        P("groups"),
        P(("groups", "col")),
    )
    return jax.shard_map(
        functools.partial(body, mesh.shape["row"], mesh.shape["col"]),
        mesh=mesh,
        in_specs=placed,
        out_specs=(P(("groups", "row"), "col"), P(("groups", "col"))),
        check_vma=False,
    )
```
